32 devices in a mesh: dom: 8 (over y, x, core), sub: 4 (over z).
Axes of the slice: x: 2, y: 2, z: 4, core: 2. Of those that a mesh axis runs over, the one named last changes fastest.
Arguments:
- dof_values: float32 [56, 9, 4096], P(None, None, ('dom', 'sub')), may hold values from -0.6 to 0.6
- stiffness: float32 [3, 56, 56], replicated, may hold values from -0.75 to 0.75
- face_project: float32 [4, 21, 56], replicated, may hold values from -0.75 to 0.75
- face_lift: float32 [4, 56, 21], replicated, may hold values from -1.25 to 1.25
- face_rotate: float32 [3, 21, 21], replicated, may hold values from -1.25 to 1.25
- star_matrices: float32 [3, 9, 9, 4096], P(None, None, None, ('dom', 'sub')), may hold values from -2 to 2
- flux_local: float32 [4, 9, 9, 4096], P(None, None, None, ('dom', 'sub')), may hold values from -1.2 to 1.2
- flux_neighbour: float32 [4, 9, 9, 4096], P(None, None, None, ('dom', 'sub')), may hold values from -1.2 to 1.2
- cluster_labels: int32 [4096], P(('dom', 'sub')), may hold values from 0 to 1, as said below
- neighbour_index: int32 [4, 4096], P(None, ('dom', 'sub')), may hold values from 0 to 287, as said below
- neighbour_face: int32 [4, 4096], P(None, ('dom', 'sub')), may hold values from 0 to 3
- neighbour_orient: int32 [4, 4096], P(None, ('dom', 'sub')), may hold values from 0 to 2
- send_element: int32 [32, 160], P(('dom', 'sub')), may hold values from 0 to 127
- send_face: int32 [32, 160], P(('dom', 'sub')), may hold values from 0 to 3
Outputs:
- new_dofs: float32 [56, 9, 4096], P(None, None, ('dom', 'sub'))
The draws below stay inside these ranges and needn't reach their ends.
Inputs may be any that keep to these rules, and one draw needn't show every extreme that they name: `cluster_labels`: 0 marks an element of the fine cluster, 1 of the coarse cluster. `neighbour_index`: values below 128 name an own element of the same device; value 128 + s names receive slot s of that device. Every receive slot of a device is named by exactly one face of that device's elements.
All inputs are finite; a program needn't handle non-finite values.
Results may differ from the reference program's by a relative error of at most 0.0001.
Values sent between devices are 32-bit elements; how exact they have to be, the bound alone decides.
No kernel may reach another device: no remote copies, remote signals or barrier semaphores. Data moves between devices by JAX's collectives and lax.ppermute only.
A program may use at most 128 MiB of HBM per device.

```python
import jax
import jax.numpy as jnp
from jax import lax

BASIS = 56
FACE_BASIS = 21
QUANTITIES = 9
TAYLOR_TERMS = 6
ELEMENTS_DEV = 128
HALO_CURVE = 64
HALO_PEER = 8
HALO_SLOTS = 160
ELEMENTS = 4096
N_DOM = 8
N_SUB = 4
DEVICES = 32


def draw_cluster_labels(key, part):
    devices = ELEMENTS // ELEMENTS_DEV
    share = jax.random.randint(jax.random.fold_in(key, 11), (devices, 1), 10, 71)
    rolls = jax.random.randint(jax.random.fold_in(key, 12), (devices, ELEMENTS_DEV), 0, 100)
    return (rolls >= share).astype(jnp.int32).reshape(ELEMENTS)


def draw_neighbour_index(key, part):
    devices = ELEMENTS // ELEMENTS_DEV
    device_keys = jax.random.split(jax.random.fold_in(key, 21), devices)

    def one_device(device_key):
        shuffled = jax.random.permutation(jax.random.fold_in(device_key, 1), 4 * ELEMENTS_DEV).astype(jnp.int32)
        locals_drawn = jax.random.randint(jax.random.fold_in(device_key, 2), (4 * ELEMENTS_DEV,), 0, ELEMENTS_DEV)
        return jnp.where(shuffled < HALO_SLOTS, ELEMENTS_DEV + shuffled, locals_drawn).astype(jnp.int32)
    table = jax.vmap(one_device)(device_keys)
    return jnp.transpose(table.reshape(devices, 4, ELEMENTS_DEV), (1, 0, 2)).reshape(4, ELEMENTS)


def place_ends(drawn, key, least, high):
    longest = drawn.shape.index(max(drawn.shape))
    spots = []
    for shift in (0, 1):
        where = [jax.random.randint(jax.random.fold_in(key, axis), (), 0, length) for axis, length in enumerate(drawn.shape)]
        where[longest] = (where[longest] + shift) % drawn.shape[longest]
        spots.append(tuple(where))
    return drawn.at[spots[0]].set(least).at[spots[1]].set(high)


def block_levels(rng, dims, cuts, smallest, top_value):
    factor_of = 1.0
    for axis_at, parts in cuts:
        heights = jax.random.uniform(jax.random.fold_in(jax.random.fold_in(rng, 6), axis_at), (parts,), jnp.float32, smallest / len(cuts), top_value / len(cuts))
        factor_of = factor_of * jnp.repeat(jnp.exp(heights), dims[axis_at] // parts).reshape((-1,) + (1,) * (len(dims) - 1 - axis_at))
    return factor_of


def noise(own_key, shape, scale, reach, cuts=(), kind=jnp.bfloat16):
    array = scale * jax.random.normal(own_key, shape, jnp.float32)
    if cuts:
        array = array * block_levels(own_key, shape, cuts, -0.22, 0.18)
    return jnp.clip(array, -reach, reach).astype(kind)


def setup_inputs(seed: int = 0) -> dict:
    key_of = jax.random.split(jax.random.key(seed), 15)
    return {
        "dof_values": noise(key_of[0], (BASIS, QUANTITIES, ELEMENTS), 0.1, 0.6, ((2, 32),), jnp.float32),
        "stiffness": noise(key_of[1], (3, BASIS, BASIS), BASIS ** -0.5, 0.75, (), jnp.float32),
        "face_project": noise(key_of[2], (4, FACE_BASIS, BASIS), BASIS ** -0.5, 0.75, (), jnp.float32),
        "face_lift": noise(key_of[3], (4, BASIS, FACE_BASIS), FACE_BASIS ** -0.5, 1.25, (), jnp.float32),
        "face_rotate": noise(key_of[4], (3, FACE_BASIS, FACE_BASIS), FACE_BASIS ** -0.5, 1.25, (), jnp.float32),
        "star_matrices": noise(key_of[5], (3, QUANTITIES, QUANTITIES, ELEMENTS), 0.33, 2.0, ((3, 32),), jnp.float32),
        "flux_local": noise(key_of[6], (4, QUANTITIES, QUANTITIES, ELEMENTS), 0.2, 1.2, ((3, 32),), jnp.float32),
        "flux_neighbour": noise(key_of[7], (4, QUANTITIES, QUANTITIES, ELEMENTS), 0.2, 1.2, ((3, 32),), jnp.float32),
        "cluster_labels": draw_cluster_labels(jax.random.fold_in(key_of[14], 71), 0),
        "neighbour_index": draw_neighbour_index(jax.random.fold_in(key_of[14], 71), 0),
        "neighbour_face": place_ends(jax.random.randint(key_of[10], (4, ELEMENTS), 0, 4), jax.random.fold_in(key_of[10], 1), 0, 3).astype(jnp.int32),
        "neighbour_orient": place_ends(jax.random.randint(key_of[11], (4, ELEMENTS), 0, 3), jax.random.fold_in(key_of[11], 1), 0, 2).astype(jnp.int32),
        "send_element": place_ends(jax.random.randint(key_of[12], (DEVICES, HALO_SLOTS), 0, ELEMENTS_DEV), jax.random.fold_in(key_of[12], 1), 0, ELEMENTS_DEV - 1).astype(jnp.int32),
        "send_face": place_ends(jax.random.randint(key_of[13], (DEVICES, HALO_SLOTS), 0, 4), jax.random.fold_in(key_of[13], 1), 0, 3).astype(jnp.int32),
    }


highest = lax.Precision.HIGHEST
step_fine = 1.0


def left_apply(matrix, values):
    rows = values.shape[0]
    flat = values.reshape(rows, -1)
    out = jnp.dot(matrix, flat, precision=highest, preferred_element_type=jnp.float32)
    return out.reshape((matrix.shape[0],) + values.shape[1:])


def mix_variables(values, mats):
    running = values[:, 0, None, :] * mats[0][None, :, :]
    for inner in range(1, values.shape[1]):
        running = running + values[:, inner, None, :] * mats[inner][None, :, :]
    return running


def derive(values, stiffness, star_matrices):
    running = None
    for direction in range(3):
        spread = left_apply(jnp.transpose(stiffness[direction]), values)
        term = mix_variables(spread, star_matrices[direction])
        running = term if running is None else running + term
    return running


def volume_part(values, stiffness, star_matrices):
    running = None
    for direction in range(3):
        spread = left_apply(stiffness[direction], values)
        term = mix_variables(spread, star_matrices[direction])
        running = term if running is None else running + term
    return running


def time_integrals(values, stiffness, star_matrices, intervals):
    running = [jnp.zeros_like(values) for interval in intervals]
    derivative = values
    factor = 1.0
    for degree in range(TAYLOR_TERMS):
        factor = factor * (degree + 1)
        running = [total + ((interval[1] ** (degree + 1) - interval[0] ** (degree + 1)) / factor) * derivative
                   for total, interval in zip(running, intervals)]
        if degree + 1 < TAYLOR_TERMS:
            derivative = derive(derivative, stiffness, star_matrices)
    return running


def face_traces(integral, face_project):
    fbasis = face_project.shape[1]
    stacked = left_apply(face_project.reshape(4 * fbasis, face_project.shape[2]), integral)
    stacked = stacked.reshape(4, fbasis, integral.shape[1], integral.shape[2])
    return jnp.transpose(stacked, (1, 2, 0, 3))


def chosen_traces(integral, chosen_elements, chosen_faces, face_project):
    picked = integral[:, :, chosen_elements]
    fbasis = face_project.shape[1]
    every = left_apply(face_project.reshape(4 * fbasis, face_project.shape[2]), picked)
    every = every.reshape(4, fbasis, picked.shape[1], picked.shape[2])
    select = (chosen_faces[None, :] == jnp.arange(4, dtype=jnp.int32)[:, None]).astype(every.dtype)
    return jnp.sum(every * select[:, None, None, :], axis=0)


def flux_sum(traces, face_lift, solvers):
    solved = jnp.stack([mix_variables(traces[:, :, face, :], solvers[face]) for face in range(4)], axis=0)
    fbasis = face_lift.shape[2]
    lift_all = jnp.transpose(face_lift, (1, 0, 2)).reshape(face_lift.shape[1], 4 * fbasis)
    return left_apply(lift_all, solved.reshape((4 * fbasis,) + solved.shape[2:]))


def rotate(traces, neighbour_orient, face_rotate):
    rotated = jnp.zeros_like(traces)
    for variant in range(3):
        chosen = (neighbour_orient == variant)[None, None, :, :]
        turned = left_apply(face_rotate[variant], traces)
        rotated = rotated + jnp.where(chosen, turned, jnp.zeros_like(turned))
    return rotated


def residual_update(integral, traces, stiffness, star_matrices, face_project, face_lift, face_rotate,
                    flux_local, flux_neighbour, neighbour_orient):
    volume = volume_part(integral, stiffness, star_matrices)
    own_flux = flux_sum(face_traces(integral, face_project), face_lift, flux_local)
    remote = flux_sum(rotate(traces, neighbour_orient, face_rotate), face_lift, flux_neighbour)
    return volume - own_flux - remote


def neighbour_traces(integral, face_project, neighbour_index, neighbour_face, send_element, send_face):
    width = integral.shape[1]
    fbasis = face_project.shape[1]
    own_all = face_traces(integral, face_project)
    owners = jnp.arange(DEVICES, dtype=jnp.int32)[:, None] * ELEMENTS_DEV
    global_elements = (owners + send_element).reshape(-1)
    sent = chosen_traces(integral, global_elements, send_face.reshape(-1), face_project)
    sent = sent.reshape(fbasis, width, N_DOM, N_SUB, HALO_SLOTS)
    blank = jnp.zeros((fbasis, width, 1, N_SUB, HALO_CURVE), sent.dtype)
    from_below = jnp.concatenate([blank, sent[:, :, :-1, :, HALO_CURVE:2 * HALO_CURVE]], axis=2)
    from_above = jnp.concatenate([sent[:, :, 1:, :, 0:HALO_CURVE], blank], axis=2)
    peers = sent[:, :, :, :, 2 * HALO_CURVE:].reshape(fbasis, width, N_DOM, N_SUB, N_SUB, HALO_PEER)
    peers = jnp.swapaxes(peers, 3, 4).reshape(fbasis, width, N_DOM, N_SUB, N_SUB * HALO_PEER)
    received = jnp.concatenate([from_below, from_above, peers], axis=4).reshape(fbasis, width, DEVICES * HALO_SLOTS)
    table = jnp.concatenate([own_all.reshape(fbasis, width, 4 * ELEMENTS), received], axis=2)
    device_of = (jnp.arange(ELEMENTS, dtype=jnp.int32) // ELEMENTS_DEV)[None, :]
    lookup = jnp.where(neighbour_index < ELEMENTS_DEV,
                       neighbour_face * ELEMENTS + device_of * ELEMENTS_DEV + neighbour_index,
                       4 * ELEMENTS + device_of * HALO_SLOTS + neighbour_index - ELEMENTS_DEV).astype(jnp.int32)
    return table[:, :, lookup]


def reference(dof_values, stiffness, face_project, face_lift, face_rotate, star_matrices, flux_local,
              flux_neighbour, cluster_labels, neighbour_index, neighbour_face, neighbour_orient,
              send_element, send_face):
    fine_mask = (cluster_labels == 0)[None, None, :]
    first, second = time_integrals(dof_values, stiffness, star_matrices,
                                   [(0.0, step_fine), (step_fine, 2.0 * step_fine)])
    traces_one = neighbour_traces(first, face_project, neighbour_index, neighbour_face, send_element, send_face)
    update_one = residual_update(first, traces_one, stiffness, star_matrices, face_project, face_lift,
                                 face_rotate, flux_local, flux_neighbour, neighbour_orient)
    middle = jnp.where(fine_mask, dof_values + update_one, dof_values)
    restart = time_integrals(middle, stiffness, star_matrices, [(0.0, step_fine)])[0]
    later = jnp.where(fine_mask, restart, second)
    traces_two = neighbour_traces(later, face_project, neighbour_index, neighbour_face, send_element, send_face)
    own_integral = jnp.where(fine_mask, later, first + second)
    fine_faces = fine_mask[:, :, None, :]
    all_traces = jnp.where(fine_faces, traces_two, traces_one + traces_two)
    start_state = jnp.where(fine_mask, middle, dof_values)
    update_two = residual_update(own_integral, all_traces, stiffness, star_matrices, face_project, face_lift,
                                 face_rotate, flux_local, flux_neighbour, neighbour_orient)
    return start_state + update_two
```

```python
import jax
import jax.numpy as jnp
from jax import lax
from jax.experimental import pallas as pl
from jax.experimental.pallas import tpu as pltpu
from jax.sharding import PartitionSpec as P

TAYLOR_TERMS = 6
HALO_CURVE = 64
HALO_PEER = 8
F32 = jnp.float32
BF16 = jnp.bfloat16
LANES = 128
KB = 64


def up(n, m):
    return -(-n // m) * m


def halves(x):
    hi = x.astype(BF16)
    return hi, (x - hi.astype(F32)).astype(BF16)


def dot(a, b):
    return jnp.dot(a, b, preferred_element_type=F32)


class Dims:
    def __init__(self, basis, nvar, elements, fbasis, slots, subs):
        self.basis, self.nvar, self.elements, self.fbasis = basis, nvar, elements, fbasis
        self.slots, self.subs = slots, subs
        self.mp = up(fbasis, 8)
        self.fm = 4 * self.mp
        self.rows = nvar * self.mp
        self.width = nvar * elements
        self.cols4 = 4 * elements
        self.slot_cols = up(slots, LANES)
        self.half = up(-(-self.rows // 2), 8)
        self.rows_pad = up(self.rows, LANES)
        self.left_rows = self.fm + 3 * basis
        self.groups = []
        r0 = 0
        while r0 < basis:
            rn = min(32, basis - r0)
            self.groups.append((r0, rn))
            r0 += rn
        self.chunks = []
        c0 = 0
        while c0 < self.width:
            cn = min(2 * elements, self.width - c0)
            self.chunks.append((c0, cn))
            c0 += cn

    def var(self, v):
        return slice(v * self.elements, (v + 1) * self.elements)


def fill_left(n, left, left_f32, pad, project, mats):
    pad[...] = jnp.zeros_like(pad)
    for m in range(n.fbasis):
        for g in range(4):
            r = g * n.mp + m
            pad[r : r + 1, : n.basis] = project[m, g : g + 1, :]
    for d in range(3):
        r = n.fm + d * n.basis
        pad[r : r + n.basis, : n.basis] = mats[d]
    w = pad[...]
    hi = w.astype(BF16).astype(F32)
    lo = w - hi
    left[:, :LANES] = (hi + pltpu.roll(lo, KB, 1)).astype(BF16)
    left[:, LANES : LANES + KB] = hi[:, :KB].astype(BF16)


def put(n, right, r0, v, x):
    rows = x.shape[0]
    if rows % 16:
        x = jnp.concatenate([x, jnp.zeros((16 - rows % 16, x.shape[1]), F32)], axis=0)
        rows = x.shape[0]
    hi, lo = halves(x)
    c = n.var(v)
    right[r0 : r0 + rows, c] = hi
    right[KB + r0 : KB + r0 + rows, c] = hi
    right[2 * KB + r0 : 2 * KB + r0 + rows, c] = lo


def mix(n, load, terms, coef):
    acc = [None] * n.nvar
    for v in range(n.nvar):
        for k in range(terms):
            t = load(v, k)
            for w in range(n.nvar):
                p = t * coef(v, w, k)
                acc[w] = p if acc[w] is None else acc[w] + p
    return acc


def spread_all(n, spread, left, right, lo_row):
    for c0, cn in n.chunks:
        spread[lo_row:, c0 : c0 + cn] = dot(left[lo_row:, :], right[:, c0 : c0 + cn])


def star_mix(n, spread, star, r0, rn):
    def load(v, d):
        r = n.fm + d * n.basis + r0
        return spread[r : r + rn, n.var(v)]

    return mix(n, load, 3, lambda v, w, d: star[v, w, d : d + 1, :])


def predict(n, left, right, spread, star, sums, weights):
    def body(k, carry):
        inv, two = carry
        kf = (k + 1).astype(F32)
        inv = inv / kf
        two = two * 2.0
        spread_all(n, spread, left, right, n.fm)
        scale = weights(inv, two)
        for r0, rn in n.groups:
            acc = star_mix(n, spread, star, r0, rn)
            for w in range(n.nvar):
                c = n.var(w)
                for field, s in zip(sums, scale):
                    field[r0 : r0 + rn, c] += s * acc[w]
                put(n, right, r0, w, acc[w])
        return inv, two

    lax.fori_loop(1, TAYLOR_TERMS, body, (jnp.float32(1.0), jnp.float32(2.0)))


def fill_right(n, right, field):
    for r0, rn in n.groups:
        for v in range(n.nvar):
            put(n, right, r0, v, field[r0 : r0 + rn, n.var(v)])


def send_onehot(n, onehot, keys, send_element, send_face):
    keys[...] = jnp.full(keys.shape, -1, jnp.int32)
    keys[0:1, : n.slots] = send_face[...] * n.elements + send_element[...]
    row = lax.broadcasted_iota(jnp.int32, onehot.shape, 0)
    onehot[...] = jnp.where(row == keys[0:1, :], 1.0, 0.0).astype(BF16)


def traces_and_sends(n, left, right, table, onehot, turned, lower, upper, peers):
    for v in range(n.nvar):
        p = dot(left[: n.fm, :], right[:, n.var(v)])
        for g in range(4):
            table[v * n.mp : (v + 1) * n.mp, n.var(g)] = p[g * n.mp : (g + 1) * n.mp]
    hi, lo = halves(table[...])
    chosen = dot(hi, onehot[...]) + dot(lo, onehot[...])
    curve = chosen[:, :LANES]
    first, rest = curve[: n.half], curve[n.half :]
    short = n.half - rest.shape[0]
    if short:
        rest = jnp.concatenate([rest, jnp.zeros((short, LANES), F32)], axis=0)
    lane = lax.broadcasted_iota(jnp.int32, first.shape, 1)
    lower[...] = jnp.where(lane < HALO_CURVE, first, pltpu.roll(rest, HALO_CURVE, 1))
    upper[...] = jnp.where(lane < HALO_CURVE, pltpu.roll(first, HALO_CURVE, 1), rest)
    turned[...] = jnp.zeros_like(turned)
    wide = jnp.concatenate([chosen[:, LANES:], jnp.zeros((n.rows_pad - n.rows, n.slot_cols - LANES), F32)], axis=0)
    turned[...] = wide.T
    here = lax.axis_index("sub")
    for k, ref in enumerate(peers):
        block = lax.rem(here + k, n.subs)
        ref[...] = turned[pl.ds(pl.multiple_of(block * HALO_PEER, HALO_PEER), HALO_PEER), :]


def first_kernel(n, dof, project, stiffness, star, send_element, send_face,
                 first, second, table, lower, upper, *rest):
    peers = rest[: n.subs]
    left, onehot, right, spread, pad, keys, turned = rest[n.subs :]
    fill_left(n, left, None, pad, project, [stiffness[d].T for d in range(3)])
    send_onehot(n, onehot, keys, send_element, send_face)
    for v in range(n.nvar):
        x = dof[v]
        first[:, n.var(v)] = x
        second[:, n.var(v)] = x
    fill_right(n, right, first)
    predict(n, left, right, spread, star, [first, second],
            lambda inv, two: [inv, (two - 1.0) * inv])
    fill_right(n, right, first)
    traces_and_sends(n, left, right, table, onehot, turned, lower, upper, peers)


def own_part(n, left, right, spread, star, flux_local, lift, solved, stacked, part):
    spread_all(n, spread, left, right, 0)
    for g in range(4):
        def load(v, k, g=g):
            return spread[g * n.mp : (g + 1) * n.mp, n.var(v)]

        acc = mix(n, load, 1, lambda v, w, k, g=g: flux_local[v, w, g : g + 1, :])
        for w in range(n.nvar):
            solved[g * n.mp : (g + 1) * n.mp, n.var(w)] = acc[w]
    for w in range(n.nvar):
        hi, lo = halves(solved[:, n.var(w)])
        stacked[: n.fm, n.var(w)] = hi
        stacked[LANES : LANES + n.fm, n.var(w)] = lo
    stacked[n.fm : LANES, :] = jnp.zeros((LANES - n.fm, n.width), BF16)
    stacked[LANES + n.fm :, :] = jnp.zeros((LANES - n.fm, n.width), BF16)
    for r0, rn in n.groups:
        acc = star_mix(n, spread, star, r0, rn)
        for w in range(n.nvar):
            part[r0 : r0 + rn, n.var(w)] = acc[w]
    for c0, cn in n.chunks:
        out = dot(lift[...], stacked[:, c0 : c0 + cn])
        part[:, c0 : c0 + cn] = part[:, c0 : c0 + cn] - (out[: n.basis] + out[n.basis :])


def lift_rows(n, out, tall, w):
    hi = w.astype(BF16).astype(F32)
    lo = w - hi
    span = w.shape[1]
    tall[: n.basis, :span] = hi
    tall[n.basis : 2 * n.basis, :span] = lo
    out[:, :span] = tall[: 2 * n.basis, :span].astype(BF16)
    tall[n.basis : 2 * n.basis, :span] = jnp.zeros_like(lo)
    out[:, span:] = tall[: 2 * n.basis, :span].astype(BF16)


def second_kernel(n, field, table, project, stiffness, star, face_lift, face_rotate, flux_local, index, face, orient,
                  part, found, left, lift, lift_turned, onehot_own, onehot_halo, masks,
                  right, spread, pad, solved, stacked, wide, tall, square, mask_rows):
    fill_left(n, left, None, pad, project, [stiffness[d] for d in range(3)])
    fill_right(n, right, field)
    wide[...] = jnp.zeros_like(wide)
    square[...] = jnp.zeros_like(square)
    for m in range(n.fbasis):
        for g in range(4):
            r = g * n.mp + m
            square[r : r + 1, : n.basis] = face_lift[m, g : g + 1, :]
    base = square[...]
    lift_rows(n, lift, tall, base.T[: n.basis, :])
    for o in range(3):
        square[...] = jnp.zeros_like(square)
        square[: n.fbasis, : n.fbasis] = face_rotate[o]
        turn = square[...].T[: n.mp, :]
        turn = turn[:, : n.mp]
        for g in range(4):
            r = o * n.fm + g * n.mp
            wide[r : r + n.mp, :] = jnp.dot(turn, base[g * n.mp : (g + 1) * n.mp, :],
                                            precision=lax.Precision.HIGHEST, preferred_element_type=F32)
    blocks = wide.shape[0] // LANES
    turned = jnp.concatenate([wide[i * LANES : (i + 1) * LANES, :].T[: n.basis, :] for i in range(blocks)], axis=1)
    lift_rows(n, lift_turned, tall, turned)
    dom = lax.axis_index("dom")
    last = lax.axis_size("dom") - 1
    for f in range(4):
        idx = index[f : f + 1, :]
        slot = idx - n.elements
        own = jnp.where(slot < 0, face[f : f + 1, :] * n.elements + idx, -1)
        slot = jnp.where(jnp.logical_and(slot < HALO_CURVE, dom == 0), -1, slot)
        high = jnp.logical_and(slot >= HALO_CURVE, slot < 2 * HALO_CURVE)
        slot = jnp.where(jnp.logical_and(high, dom == last), -1, slot)
        row = lax.broadcasted_iota(jnp.int32, (n.cols4, n.elements), 0)
        onehot_own[:, n.var(f)] = jnp.where(row == own, 1.0, 0.0).astype(BF16)
        row = lax.broadcasted_iota(jnp.int32, (n.slot_cols, n.elements), 0)
        onehot_halo[:, n.var(f)] = jnp.where(row == slot, 1.0, 0.0).astype(BF16)
        for o in range(3):
            r = o * n.fm + f * n.mp
            mask_rows[r : r + n.mp, :] = jnp.broadcast_to(
                jnp.where(orient[f : f + 1, :] == o, 1.0, 0.0), (n.mp, n.elements))
    masks[...] = mask_rows[...].astype(BF16)
    own_part(n, left, right, spread, star, flux_local, lift, solved, stacked, part)
    hi, lo = halves(table[...])
    found[...] = dot(hi, onehot_own[...]) + dot(lo, onehot_own[...])


def neighbour_part(n, below, above, peers, found, onehot_halo, flux_neighbour, masks, lift_turned,
                   traces, solved, stacked, turned):
    lane = lax.broadcasted_iota(jnp.int32, below.shape, 1)
    b, a = below[...], above[...]
    first = jnp.where(lane < HALO_CURVE, b, pltpu.roll(a, HALO_CURVE, 1))
    rest = jnp.where(lane < HALO_CURVE, pltpu.roll(b, HALO_CURVE, 1), a)
    curve = jnp.concatenate([first, rest], axis=0)[: n.rows]
    turned[...] = jnp.zeros_like(turned)
    here = lax.axis_index("sub")
    for k, ref in enumerate(peers):
        block = lax.rem(here + n.subs - k, n.subs)
        turned[pl.ds(pl.multiple_of(block * HALO_PEER, HALO_PEER), HALO_PEER), :] = ref[...]
    flat = turned[...].T[: n.rows, :]
    hi, lo = halves(jnp.concatenate([curve, flat], axis=1))
    traces[...] = found[...] + dot(hi, onehot_halo[...]) + dot(lo, onehot_halo[...])
    for f in range(4):
        def load(v, k, f=f):
            return traces[v * n.mp : (v + 1) * n.mp, n.var(f)]

        acc = mix(n, load, 1, lambda v, w, k, f=f: flux_neighbour[v, w, f : f + 1, :])
        for w in range(n.nvar):
            solved[f * n.mp : (f + 1) * n.mp, n.var(w)] = acc[w]
    span = stacked.shape[0] // 2
    for w in range(n.nvar):
        hi, lo = halves(solved[:, n.var(w)])
        for o in range(3):
            m = masks[o * n.fm : (o + 1) * n.fm, :]
            stacked[o * n.fm : (o + 1) * n.fm, n.var(w)] = hi * m
            stacked[span + o * n.fm : span + (o + 1) * n.fm, n.var(w)] = lo * m
    gap = span - 3 * n.fm
    if gap:
        stacked[3 * n.fm : span, :] = jnp.zeros((gap, n.width), BF16)
        stacked[span + 3 * n.fm :, :] = jnp.zeros((gap, n.width), BF16)


def third_kernel(n, *refs):
    below, above = refs[:2]
    peers = refs[2 : 2 + n.subs]
    (found, onehot_halo, flux_neighbour, masks, lift_turned, part, dof, labels, second, star, left, send_onehot_ref,
     later, middle, traces, table, lower, upper) = refs[2 + n.subs : 20 + n.subs]
    sent = refs[20 + n.subs : 20 + 2 * n.subs]
    right, spread, solved, stacked, turned = refs[20 + 2 * n.subs :]
    neighbour_part(n, below, above, peers, found, onehot_halo, flux_neighbour, masks, lift_turned,
                   traces, solved, stacked, turned)
    fine = labels[...] == 0
    for c0, cn in n.chunks:
        out = dot(lift_turned[...], stacked[:, c0 : c0 + cn])
        nb = out[: n.basis] + out[n.basis :]
        for v in range(c0 // n.elements, (c0 + cn) // n.elements):
            c = n.var(v)
            o = v * n.elements - c0
            x = dof[v]
            mid = jnp.where(fine, x + (part[:, c] - nb[:, o : o + n.elements]), x)
            middle[:, c] = mid
            later[:, c] = mid
    fill_right(n, right, middle)
    predict(n, left, right, spread, star, [later], lambda inv, two: [inv])
    for v in range(n.nvar):
        c = n.var(v)
        later[:, c] = jnp.where(fine, later[:, c], second[:, c])
    fill_right(n, right, later)
    traces_and_sends(n, left, right, table, send_onehot_ref, turned, lower, upper, sent)


def fourth_kernel(n, first, second, later, middle, labels, star, left, flux_local, lift, table, onehot_own, traces,
                  part, found, right, spread, solved, stacked):
    fine = labels[...] == 0
    for r0, rn in n.groups:
        for v in range(n.nvar):
            c = n.var(v)
            rows = slice(r0, r0 + rn)
            put(n, right, r0, v, jnp.where(fine, later[rows, c], first[rows, c] + second[rows, c]))
    own_part(n, left, right, spread, star, flux_local, lift, solved, stacked, part)
    part[...] = middle[...] + part[...]
    hi, lo = halves(table[...])
    got = dot(hi, onehot_own[...]) + dot(lo, onehot_own[...])
    for f in range(4):
        c = n.var(f)
        found[:, c] = got[:, c] + jnp.where(fine, 0.0, traces[:, c])


def fifth_kernel(n, *refs):
    below, above = refs[:2]
    peers = refs[2 : 2 + n.subs]
    found, onehot_halo, flux_neighbour, masks, lift_turned, part, out, traces, solved, stacked, turned = refs[2 + n.subs :]
    neighbour_part(n, below, above, peers, found, onehot_halo, flux_neighbour, masks, lift_turned,
                   traces, solved, stacked, turned)
    for c0, cn in n.chunks:
        got = dot(lift_turned[...], stacked[:, c0 : c0 + cn])
        nb = got[: n.basis] + got[n.basis :]
        for v in range(c0 // n.elements, (c0 + cn) // n.elements):
            o = v * n.elements - c0
            out[v] = part[:, n.var(v)] - nb[:, o : o + n.elements]


def call(kernel, n, operands, outs, scratch, name):
    vm = pl.BlockSpec(memory_space=pltpu.VMEM)

    def body(*refs):
        kernel(n, *refs)

    return pl.pallas_call(
        body,
        out_shape=[jax.ShapeDtypeStruct(s, t) for s, t in outs],
        in_specs=[vm] * len(operands),
        out_specs=[vm] * len(outs),
        scratch_shapes=[pltpu.VMEM(s, t) for s, t in scratch],
        name=name,
    )(*operands)


def ring(value, axis, by):
    peers = lax.axis_size(axis)
    return lax.ppermute(value, axis, [(i, (i + by) % peers) for i in range(peers)])


def exchange(lower, upper, peers):
    below = ring(upper, "dom", 1)
    above = ring(lower, "dom", -1)
    return [below, above, peers[0]] + [ring(p, "sub", k) for k, p in enumerate(peers) if k]


def per_device(dof_values, stiffness, face_project, face_lift, face_rotate, star_matrices, flux_local, flux_neighbour,
               cluster_labels, neighbour_index, neighbour_face, neighbour_orient, send_element, send_face):
    n = Dims(dof_values.shape[0], dof_values.shape[1], dof_values.shape[2], face_project.shape[1],
             send_element.shape[1], lax.axis_size("sub"))
    dof = jnp.transpose(dof_values, (1, 0, 2))
    star = jnp.transpose(star_matrices, (1, 2, 0, 3))
    local = jnp.transpose(flux_local, (1, 2, 0, 3))
    remote = jnp.transpose(flux_neighbour, (1, 2, 0, 3))
    project = jnp.transpose(face_project, (1, 0, 2))
    lift = jnp.transpose(face_lift, (2, 0, 1))
    labels = cluster_labels.reshape(1, n.elements)

    field = ((n.basis, n.width), F32)
    grid = ((n.rows, n.cols4), F32)
    pack = ((n.half, LANES), F32)
    peer = ((HALO_PEER, n.rows_pad), F32)
    left_t = ((n.left_rows, 3 * KB), BF16)
    right_t = ((3 * KB, n.width), BF16)
    spread_t = ((n.left_rows, n.width), F32)
    turned_t = ((n.slot_cols - LANES, n.rows_pad), F32)
    solved_t = ((n.fm, n.width), F32)
    own_stack = ((2 * LANES, n.width), BF16)
    rot_rows = up(3 * n.fm, LANES)
    rot_stack = ((2 * rot_rows, n.width), BF16)
    pad_t = ((n.left_rows, LANES), F32)

    outs = call(
        first_kernel, n, [dof, project, stiffness, star, send_element, send_face],
        [field, field, grid, pack, pack] + [peer] * n.subs + [left_t, ((n.cols4, n.slot_cols), BF16)],
        [right_t, spread_t, pad_t, ((8, n.slot_cols), jnp.int32), turned_t], "predict_first")
    first, second, table, lower, upper = outs[:5]
    peers = outs[5 : 5 + n.subs]
    left_one, send_sel = outs[5 + n.subs :]
    got = exchange(lower, upper, peers)
    part, found, left_two, lift_own, lift_rot, sel_own, sel_halo, masks = call(
        second_kernel, n,
        [first, table, project, stiffness, star, lift, face_rotate, local, neighbour_index, neighbour_face, neighbour_orient],
        [field, grid, left_t, ((2 * n.basis, 2 * LANES), BF16), ((2 * n.basis, 2 * rot_rows), BF16),
         ((n.cols4, n.cols4), BF16), ((n.slot_cols, n.cols4), BF16), ((3 * n.fm, n.elements), BF16)],
        [right_t, spread_t, pad_t, solved_t, own_stack, ((rot_rows, LANES), F32), ((2 * n.basis, rot_rows), F32),
         ((LANES, LANES), F32), ((3 * n.fm, n.elements), F32)], "own_first")
    outs = call(
        third_kernel, n,
        got + [found, sel_halo, remote, masks, lift_rot, part, dof, labels, second, star, left_one, send_sel],
        [field, field, grid, grid, pack, pack] + [peer] * n.subs,
        [right_t, spread_t, solved_t, rot_stack, turned_t], "neighbour_first")
    later, middle, traces, table, lower, upper = outs[:6]
    got = exchange(lower, upper, outs[6:])
    part, found = call(
        fourth_kernel, n,
        [first, second, later, middle, labels, star, left_two, local, lift_own, table, sel_own, traces],
        [field, grid], [right_t, spread_t, solved_t, own_stack], "own_second")
    (out,) = call(
        fifth_kernel, n, got + [found, sel_halo, remote, masks, lift_rot, part],
        [((n.nvar, n.basis, n.elements), F32)], [grid, solved_t, rot_stack, turned_t], "neighbour_second")
    return jnp.transpose(out, (1, 0, 2))


def solution(mesh):
    cells = ("dom", "sub")
    in_specs = (
        P(None, None, cells),
        P(),
        P(),
        P(),
        P(),
        P(None, None, None, cells),
        P(None, None, None, cells),
        P(None, None, None, cells),
        P(cells),
        P(None, cells),
        P(None, cells),
        P(None, cells),
        P(cells, None),
        P(cells, None),
    )
    out_specs = P(None, None, cells)
    return jax.shard_map(per_device, mesh=mesh, in_specs=in_specs, out_specs=out_specs, check_vma=False)
```

```python
import jax
import jax.numpy as jnp
from jax import lax
from jax.experimental import pallas as pl
from jax.experimental.pallas import tpu as pltpu
from jax.sharding import PartitionSpec as P

TAYLOR_TERMS = 6
HALO_CURVE = 64
HALO_PEER = 8
F32 = jnp.float32
BF16 = jnp.bfloat16
LANES = 128
FAR = 14
KB = 64


def up(n, m):
    return -(-n // m) * m


def halves(x):
    hi = x.astype(BF16)
    return hi, (x - hi.astype(F32)).astype(BF16)


def dot(a, b):
    return jnp.dot(a, b, preferred_element_type=F32)


class Dims:
    def __init__(self, basis, nvar, elements, fbasis, slots, subs):
        self.basis, self.nvar, self.elements, self.fbasis = basis, nvar, elements, fbasis
        self.slots, self.subs = slots, subs
        self.mp = up(fbasis, 8)
        self.fm = 4 * self.mp
        self.rows = nvar * self.mp
        self.width = nvar * elements
        self.cols4 = 4 * elements
        self.slot_cols = up(slots, LANES)
        self.half = up(-(-self.rows // 2), 8)
        self.rows_pad = up(self.rows, LANES)
        self.left_rows = self.fm + 3 * basis
        self.groups = []
        r0 = 0
        while r0 < basis:
            rn = min(32, basis - r0)
            self.groups.append((r0, rn))
            r0 += rn
        self.chunks = []
        c0 = 0
        while c0 < self.width:
            cn = min(2 * elements, self.width - c0)
            self.chunks.append((c0, cn))
            c0 += cn

    def var(self, v):
        return slice(v * self.elements, (v + 1) * self.elements)


def fill_left(n, left, left_f32, pad, project, mats):
    pad[...] = jnp.zeros_like(pad)
    for m in range(n.fbasis):
        for g in range(4):
            r = g * n.mp + m
            pad[r : r + 1, : n.basis] = project[m, g : g + 1, :]
    for d in range(3):
        r = n.fm + d * n.basis
        pad[r : r + n.basis, : n.basis] = mats[d]
    w = pad[...]
    hi = w.astype(BF16).astype(F32)
    lo = w - hi
    left[:, :LANES] = (hi + pltpu.roll(lo, KB, 1)).astype(BF16)
    left[:, LANES : LANES + KB] = hi[:, :KB].astype(BF16)


def put(n, right, r0, v, x):
    rows = x.shape[0]
    if rows % 16:
        x = jnp.concatenate([x, jnp.zeros((16 - rows % 16, x.shape[1]), F32)], axis=0)
        rows = x.shape[0]
    hi, lo = halves(x)
    c = n.var(v)
    right[r0 : r0 + rows, c] = hi
    right[KB + r0 : KB + r0 + rows, c] = hi
    right[2 * KB + r0 : 2 * KB + r0 + rows, c] = lo


def mix(n, load, terms, coef):
    acc = [None] * n.nvar
    for v in range(n.nvar):
        for k in range(terms):
            t = load(v, k)
            for w in range(n.nvar):
                p = t * coef(v, w, k)
                acc[w] = p if acc[w] is None else acc[w] + p
    return acc


def spread_all(n, spread, left, right, lo_row):
    for c0, cn in n.chunks:
        spread[lo_row:, c0 : c0 + cn] = dot(left[lo_row:, :], right[:, c0 : c0 + cn])


def star_mix(n, spread, star, r0, rn):
    def load(v, d):
        r = n.fm + d * n.basis + r0
        return spread[r : r + rn, n.var(v)]

    return mix(n, load, 3, lambda v, w, d: star[v, w, d : d + 1, :])


def predict(n, left, right, spread, star, sums, weights):
    def body(k, carry):
        inv, two = carry
        kf = (k + 1).astype(F32)
        inv = inv / kf
        two = two * 2.0
        spread_all(n, spread, left, right, n.fm)
        scale = weights(inv, two)
        for r0, rn in n.groups:
            acc = star_mix(n, spread, star, r0, rn)
            for w in range(n.nvar):
                c = n.var(w)
                for field, s in zip(sums, scale):
                    field[r0 : r0 + rn, c] += s * acc[w]
                put(n, right, r0, w, acc[w])
        return inv, two

    lax.fori_loop(1, TAYLOR_TERMS, body, (jnp.float32(1.0), jnp.float32(2.0)))


def fill_right(n, right, field):
    for r0, rn in n.groups:
        for v in range(n.nvar):
            put(n, right, r0, v, field[r0 : r0 + rn, n.var(v)])


def send_onehot(n, onehot, keys, send_element, send_face):
    keys[...] = jnp.full(keys.shape, -1, jnp.int32)
    keys[0:1, : n.slots] = send_face[...] * n.elements + send_element[...]
    row = lax.broadcasted_iota(jnp.int32, onehot.shape, 0)
    onehot[...] = jnp.where(row == keys[0:1, :], 1.0, 0.0).astype(BF16)


def traces_and_sends(n, left, right, table, onehot, turned, near, far, peers):
    for v in range(n.nvar):
        p = dot(left[: n.fm, :], right[:, n.var(v)])
        for g in range(4):
            table[v * n.mp : (v + 1) * n.mp, n.var(g)] = p[g * n.mp : (g + 1) * n.mp]
    hi, lo = halves(table[...])
    chosen = dot(hi, onehot[...]) + dot(lo, onehot[...])
    curve = chosen[:, :LANES]
    first, rest = curve[: n.half], curve[n.half :]
    short = n.half - rest.shape[0]
    if short:
        rest = jnp.concatenate([rest, jnp.zeros((short, LANES), F32)], axis=0)
    lane = lax.broadcasted_iota(jnp.int32, first.shape, 1)
    lower = jnp.where(lane < HALO_CURVE, first, pltpu.roll(rest, HALO_CURVE, 1))
    upper = jnp.where(lane < HALO_CURVE, pltpu.roll(first, HALO_CURVE, 1), rest)
    even = jnp.full(first.shape, lax.rem(lax.axis_index("dom"), 2), jnp.int32) == 0
    near[...] = jnp.where(even, upper, lower)
    far[...] = jnp.where(even, lower, upper)
    turned[...] = jnp.zeros_like(turned)
    wide = jnp.concatenate([chosen[:, LANES:], jnp.zeros((n.rows_pad - n.rows, n.slot_cols - LANES), F32)], axis=0)
    turned[...] = wide.T
    for k, ref in enumerate(peers):
        block = peer_block(n, k, False)
        ref[...] = turned[pl.ds(pl.multiple_of(block * HALO_PEER, HALO_PEER), HALO_PEER), :]


def first_kernel(n, *refs):
    brought = refs[:FAR]
    first, second, table, near, far = refs[FAR : FAR + 5]
    peers = refs[FAR + 5 : FAR + 5 + n.subs]
    left, onehot = refs[FAR + 5 + n.subs : FAR + 7 + n.subs]
    kept = refs[FAR + 7 + n.subs : 2 * FAR + 5 + n.subs]
    right, spread, pad, keys, turned, send_element, send_face, arrived = refs[2 * FAR + 5 + n.subs :]
    copies = [pltpu.make_async_copy(src, dst, arrived.at[i])
              for i, (src, dst) in enumerate(zip(brought, (send_element, send_face) + tuple(kept)))]
    for c in copies:
        c.start()
    project, stiffness, dof, star = kept[:4]
    for c in copies[:5]:
        c.wait()
    send_onehot(n, onehot, keys, send_element, send_face)
    fill_left(n, left, None, pad, project, [stiffness[d].T for d in range(3)])
    for v in range(n.nvar):
        x = dof[v]
        first[:, n.var(v)] = x
        second[:, n.var(v)] = x
    fill_right(n, right, first)
    copies[5].wait()
    predict(n, left, right, spread, star, [first, second],
            lambda inv, two: [inv, (two - 1.0) * inv])
    fill_right(n, right, first)
    traces_and_sends(n, left, right, table, onehot, turned, near, far, peers)
    for c in copies[6:]:
        c.wait()


def own_part(n, left, right, spread, star, flux_local, lift, solved, stacked, part):
    spread_all(n, spread, left, right, 0)
    for g in range(4):
        def load(v, k, g=g):
            return spread[g * n.mp : (g + 1) * n.mp, n.var(v)]

        acc = mix(n, load, 1, lambda v, w, k, g=g: flux_local[v, w, g : g + 1, :])
        for w in range(n.nvar):
            solved[g * n.mp : (g + 1) * n.mp, n.var(w)] = acc[w]
    for w in range(n.nvar):
        hi, lo = halves(solved[:, n.var(w)])
        stacked[: n.fm, n.var(w)] = hi
        stacked[LANES : LANES + n.fm, n.var(w)] = lo
    stacked[n.fm : LANES, :] = jnp.zeros((LANES - n.fm, n.width), BF16)
    stacked[LANES + n.fm :, :] = jnp.zeros((LANES - n.fm, n.width), BF16)
    for r0, rn in n.groups:
        acc = star_mix(n, spread, star, r0, rn)
        for w in range(n.nvar):
            part[r0 : r0 + rn, n.var(w)] = acc[w]
    for c0, cn in n.chunks:
        out = dot(lift[...], stacked[:, c0 : c0 + cn])
        part[:, c0 : c0 + cn] = part[:, c0 : c0 + cn] - (out[: n.basis] + out[n.basis :])


def lift_rows(n, out, tall, w):
    hi = w.astype(BF16).astype(F32)
    lo = w - hi
    span = w.shape[1]
    tall[: n.basis, :span] = hi
    tall[n.basis : 2 * n.basis, :span] = lo
    out[:, :span] = tall[: 2 * n.basis, :span].astype(BF16)
    tall[n.basis : 2 * n.basis, :span] = jnp.zeros_like(lo)
    out[:, span:] = tall[: 2 * n.basis, :span].astype(BF16)


def second_kernel(n, field, table, project, stiffness, star, face_lift, face_rotate, flux_local, index, face, orient,
                  part, found, left, lift, lift_turned, onehot_own, onehot_halo, masks,
                  right, spread, pad, solved, stacked, wide, tall, square, mask_rows):
    fill_left(n, left, None, pad, project, [stiffness[d] for d in range(3)])
    fill_right(n, right, field)
    wide[...] = jnp.zeros_like(wide)
    square[...] = jnp.zeros_like(square)
    for m in range(n.fbasis):
        for g in range(4):
            r = g * n.mp + m
            square[r : r + 1, : n.basis] = face_lift[m, g : g + 1, :]
    base = square[...]
    lift_rows(n, lift, tall, base.T[: n.basis, :])
    for o in range(3):
        square[...] = jnp.zeros_like(square)
        square[: n.fbasis, : n.fbasis] = face_rotate[o]
        turn = square[...].T[: n.mp, :]
        turn = turn[:, : n.mp]
        for g in range(4):
            r = o * n.fm + g * n.mp
            wide[r : r + n.mp, :] = jnp.dot(turn, base[g * n.mp : (g + 1) * n.mp, :],
                                            precision=lax.Precision.HIGHEST, preferred_element_type=F32)
    blocks = wide.shape[0] // LANES
    turned = jnp.concatenate([wide[i * LANES : (i + 1) * LANES, :].T[: n.basis, :] for i in range(blocks)], axis=1)
    lift_rows(n, lift_turned, tall, turned)
    dom = lax.axis_index("dom")
    last = lax.axis_size("dom") - 1
    for f in range(4):
        idx = index[f : f + 1, :]
        slot = idx - n.elements
        own = jnp.where(slot < 0, face[f : f + 1, :] * n.elements + idx, -1)
        slot = jnp.where(jnp.logical_and(slot < HALO_CURVE, dom == 0), -1, slot)
        high = jnp.logical_and(slot >= HALO_CURVE, slot < 2 * HALO_CURVE)
        slot = jnp.where(jnp.logical_and(high, dom == last), -1, slot)
        row = lax.broadcasted_iota(jnp.int32, (n.cols4, n.elements), 0)
        onehot_own[:, n.var(f)] = jnp.where(row == own, 1.0, 0.0).astype(BF16)
        row = lax.broadcasted_iota(jnp.int32, (n.slot_cols, n.elements), 0)
        onehot_halo[:, n.var(f)] = jnp.where(row == slot, 1.0, 0.0).astype(BF16)
        for o in range(3):
            r = o * n.fm + f * n.mp
            mask_rows[r : r + n.mp, :] = jnp.broadcast_to(
                jnp.where(orient[f : f + 1, :] == o, 1.0, 0.0), (n.mp, n.elements))
    masks[...] = mask_rows[...].astype(BF16)
    own_part(n, left, right, spread, star, flux_local, lift, solved, stacked, part)
    hi, lo = halves(table[...])
    found[...] = dot(hi, onehot_own[...]) + dot(lo, onehot_own[...])


def neighbour_part(n, near, far, peers, found, onehot_halo, flux_neighbour, masks, lift_turned,
                   traces, solved, stacked, turned):
    lane = lax.broadcasted_iota(jnp.int32, near.shape, 1)
    even = jnp.full(near.shape, lax.rem(lax.axis_index("dom"), 2), jnp.int32) == 0
    b = jnp.where(even, far[...], near[...])
    a = jnp.where(even, near[...], far[...])
    first = jnp.where(lane < HALO_CURVE, b, pltpu.roll(a, HALO_CURVE, 1))
    rest = jnp.where(lane < HALO_CURVE, pltpu.roll(b, HALO_CURVE, 1), a)
    curve = jnp.concatenate([first, rest], axis=0)[: n.rows]
    turned[...] = jnp.zeros_like(turned)
    for k, ref in enumerate(peers):
        block = peer_block(n, k, True)
        turned[pl.ds(pl.multiple_of(block * HALO_PEER, HALO_PEER), HALO_PEER), :] = ref[...]
    flat = turned[...].T[: n.rows, :]
    hi, lo = halves(jnp.concatenate([curve, flat], axis=1))
    traces[...] = found[...] + dot(hi, onehot_halo[...]) + dot(lo, onehot_halo[...])
    for f in range(4):
        def load(v, k, f=f):
            return traces[v * n.mp : (v + 1) * n.mp, n.var(f)]

        acc = mix(n, load, 1, lambda v, w, k, f=f: flux_neighbour[v, w, f : f + 1, :])
        for w in range(n.nvar):
            solved[f * n.mp : (f + 1) * n.mp, n.var(w)] = acc[w]
    span = stacked.shape[0] // 2
    for w in range(n.nvar):
        hi, lo = halves(solved[:, n.var(w)])
        for o in range(3):
            m = masks[o * n.fm : (o + 1) * n.fm, :]
            stacked[o * n.fm : (o + 1) * n.fm, n.var(w)] = hi * m
            stacked[span + o * n.fm : span + (o + 1) * n.fm, n.var(w)] = lo * m
    gap = span - 3 * n.fm
    if gap:
        stacked[3 * n.fm : span, :] = jnp.zeros((gap, n.width), BF16)
        stacked[span + 3 * n.fm :, :] = jnp.zeros((gap, n.width), BF16)


def third_kernel(n, *refs):
    near, far = refs[:2]
    peers = refs[2 : 2 + n.subs]
    (found, onehot_halo, flux_neighbour, masks, lift_turned, part, dof, labels, second, star, left, send_onehot_ref,
     later, middle, traces, table, near_out, far_out) = refs[2 + n.subs : 20 + n.subs]
    sent = refs[20 + n.subs : 20 + 2 * n.subs]
    right, spread, solved, stacked, turned = refs[20 + 2 * n.subs :]
    neighbour_part(n, near, far, peers, found, onehot_halo, flux_neighbour, masks, lift_turned,
                   traces, solved, stacked, turned)
    fine = labels[...] == 0
    for c0, cn in n.chunks:
        out = dot(lift_turned[...], stacked[:, c0 : c0 + cn])
        nb = out[: n.basis] + out[n.basis :]
        for v in range(c0 // n.elements, (c0 + cn) // n.elements):
            c = n.var(v)
            o = v * n.elements - c0
            x = dof[v]
            mid = jnp.where(fine, x + (part[:, c] - nb[:, o : o + n.elements]), x)
            middle[:, c] = mid
            later[:, c] = mid
    fill_right(n, right, middle)
    predict(n, left, right, spread, star, [later], lambda inv, two: [inv])
    for v in range(n.nvar):
        c = n.var(v)
        later[:, c] = jnp.where(fine, later[:, c], second[:, c])
    fill_right(n, right, later)
    traces_and_sends(n, left, right, table, send_onehot_ref, turned, near_out, far_out, sent)


def fourth_kernel(n, first, second, later, middle, labels, star, left, flux_local, lift, table, onehot_own, traces,
                  part, found, right, spread, solved, stacked):
    fine = labels[...] == 0
    for r0, rn in n.groups:
        for v in range(n.nvar):
            c = n.var(v)
            rows = slice(r0, r0 + rn)
            put(n, right, r0, v, jnp.where(fine, later[rows, c], first[rows, c] + second[rows, c]))
    own_part(n, left, right, spread, star, flux_local, lift, solved, stacked, part)
    part[...] = middle[...] + part[...]
    hi, lo = halves(table[...])
    got = dot(hi, onehot_own[...]) + dot(lo, onehot_own[...])
    for f in range(4):
        c = n.var(f)
        found[:, c] = got[:, c] + jnp.where(fine, 0.0, traces[:, c])


def fifth_kernel(n, *refs):
    near, far = refs[:2]
    peers = refs[2 : 2 + n.subs]
    (found, onehot_halo, flux_neighbour, masks, lift_turned, part, out,
     traces, solved, stacked, turned, result, left_for) = refs[2 + n.subs :]
    neighbour_part(n, near, far, peers, found, onehot_halo, flux_neighbour, masks, lift_turned,
                   traces, solved, stacked, turned)
    copies = []
    for c0, cn in n.chunks:
        got = dot(lift_turned[...], stacked[:, c0 : c0 + cn])
        nb = got[: n.basis] + got[n.basis :]
        for v in range(c0 // n.elements, (c0 + cn) // n.elements):
            o = v * n.elements - c0
            result[v] = part[:, n.var(v)] - nb[:, o : o + n.elements]
            copies.append(pltpu.make_async_copy(result.at[v], out.at[v], left_for.at[v]))
            copies[-1].start()
    for c in copies:
        c.wait()


def call(kernel, n, operands, outs, scratch, name, far_in=False, far_out=False):
    near, far = pltpu.VMEM, pltpu.HBM
    place = far if far_in else near

    def body(*refs):
        kernel(n, *refs)

    return pl.pallas_call(
        body,
        out_shape=[(far if far_out else near)(s, t) for s, t in outs],
        in_specs=[pl.BlockSpec(memory_space=place)] * len(operands),
        out_specs=[pl.BlockSpec(memory_space=far if far_out else near)] * len(outs),
        scratch_shapes=scratch,
        compiler_params=pltpu.CompilerParams(vmem_limit_bytes=24 << 20),
        name=name,
    )(*[pltpu.with_memory_space_constraint(x, place) for x in operands])


def along(value, axis, partner):
    count = lax.axis_size(axis)
    pairs = [(i, partner(i)) for i in range(count)]
    return lax.ppermute(value, axis, [(i, j if 0 <= j < count else i) for i, j in pairs])


def exchange(near, far, peers):
    count = lax.axis_size("sub")
    swaps = count & (count - 1) == 0
    got = [along(p, "sub", lambda i, k=k: i ^ k if swaps else (i + k) % count) for k, p in enumerate(peers) if k]
    far = along(far, "dom", lambda i: i + 1 if i % 2 else i - 1)
    near = along(near, "dom", lambda i: i ^ 1)
    return [near, far, peers[0]] + got


def peer_block(n, k, back):
    here = lax.axis_index("sub")
    if n.subs & (n.subs - 1) == 0:
        return here ^ k
    return lax.rem(here + (n.subs - k if back else k), n.subs)


def per_device(dof_values, stiffness, face_project, face_lift, face_rotate, star_matrices, flux_local, flux_neighbour,
               cluster_labels, neighbour_index, neighbour_face, neighbour_orient, send_element, send_face):
    n = Dims(dof_values.shape[0], dof_values.shape[1], dof_values.shape[2], face_project.shape[1],
             send_element.shape[1], lax.axis_size("sub"))
    dof = jnp.transpose(dof_values, (1, 0, 2))
    star = jnp.transpose(star_matrices, (1, 2, 0, 3))
    local = jnp.transpose(flux_local, (1, 2, 0, 3))
    remote = jnp.transpose(flux_neighbour, (1, 2, 0, 3))
    project = jnp.transpose(face_project, (1, 0, 2))
    lift = jnp.transpose(face_lift, (2, 0, 1))
    labels = cluster_labels.reshape(1, n.elements)

    field = ((n.basis, n.width), F32)
    grid = ((n.rows, n.cols4), F32)
    pack = ((n.half, LANES), F32)
    peer = ((HALO_PEER, n.rows_pad), F32)
    left_t = ((n.left_rows, 3 * KB), BF16)
    rot_rows = up(3 * n.fm, LANES)
    right_t = pltpu.VMEM((3 * KB, n.width), BF16)
    spread_t = pltpu.VMEM((n.left_rows, n.width), F32)
    turned_t = pltpu.VMEM((n.slot_cols - LANES, n.rows_pad), F32)
    solved_t = pltpu.VMEM((n.fm, n.width), F32)
    own_stack = pltpu.VMEM((2 * LANES, n.width), BF16)
    rot_stack = pltpu.VMEM((2 * rot_rows, n.width), BF16)
    pad_t = pltpu.VMEM((n.left_rows, LANES), F32)

    sends = [send_element, send_face]
    kept = [project, stiffness, dof, star, lift, face_rotate, local, remote, labels,
            neighbour_index, neighbour_face, neighbour_orient]
    outs = call(
        first_kernel, n, sends + kept,
        [field, field, grid, pack, pack] + [peer] * n.subs + [left_t, ((n.cols4, n.slot_cols), BF16)]
        + [(x.shape, x.dtype) for x in kept],
        [right_t, spread_t, pad_t, pltpu.VMEM((8, n.slot_cols), jnp.int32), turned_t]
        + [pltpu.VMEM(x.shape, x.dtype) for x in sends] + [pltpu.SemaphoreType.DMA((FAR,))],
        "predict_first", far_in=True)
    first, second, table, near, far = outs[:5]
    peers = outs[5 : 5 + n.subs]
    left_one, send_sel = outs[5 + n.subs : 7 + n.subs]
    project, stiffness, dof, star, lift, face_rotate, local, remote, labels, index, face, orient = outs[7 + n.subs :]
    got = exchange(near, far, peers)
    part, found, left_two, lift_own, lift_rot, sel_own, sel_halo, masks = call(
        second_kernel, n,
        [first, table, project, stiffness, star, lift, face_rotate, local, index, face, orient],
        [field, grid, left_t, ((2 * n.basis, 2 * LANES), BF16), ((2 * n.basis, 2 * rot_rows), BF16),
         ((n.cols4, n.cols4), BF16), ((n.slot_cols, n.cols4), BF16), ((3 * n.fm, n.elements), BF16)],
        [right_t, spread_t, pad_t, solved_t, own_stack]
        + [pltpu.VMEM(s, F32) for s in ((rot_rows, LANES), (2 * n.basis, rot_rows), (LANES, LANES), (3 * n.fm, n.elements))],
        "own_first")
    outs = call(
        third_kernel, n,
        got + [found, sel_halo, remote, masks, lift_rot, part, dof, labels, second, star, left_one, send_sel],
        [field, field, grid, grid, pack, pack] + [peer] * n.subs,
        [right_t, spread_t, solved_t, rot_stack, turned_t], "neighbour_first")
    later, middle, traces, table, near, far = outs[:6]
    got = exchange(near, far, outs[6:])
    part, found = call(
        fourth_kernel, n,
        [first, second, later, middle, labels, star, left_two, local, lift_own, table, sel_own, traces],
        [field, grid], [right_t, spread_t, solved_t, own_stack], "own_second")
    (out,) = call(
        fifth_kernel, n, got + [found, sel_halo, remote, masks, lift_rot, part],
        [((n.nvar, n.basis, n.elements), F32)],
        [pltpu.VMEM(*grid), solved_t, rot_stack, turned_t, pltpu.VMEM((n.nvar, n.basis, n.elements), F32),
         pltpu.SemaphoreType.DMA((n.nvar,))], "neighbour_second", far_out=True)
    return jnp.transpose(out, (1, 0, 2))


def solution(mesh):
    cells = ("dom", "sub")
    in_specs = (
        P(None, None, cells),
        P(),
        P(),
        P(),
        P(),
        P(None, None, None, cells),
        P(None, None, None, cells),
        P(None, None, None, cells),
        P(cells),
        P(None, cells),
        P(None, cells),
        P(None, cells),
        P(cells, None),
        P(cells, None),
    )
    out_specs = P(None, None, cells)
    return jax.shard_map(per_device, mesh=mesh, in_specs=in_specs, out_specs=out_specs, check_vma=False)
```

```python
import jax
import jax.numpy as jnp
from jax import lax
from jax.experimental import pallas as pl
from jax.experimental.pallas import tpu as pltpu
from jax.sharding import PartitionSpec as P


TAYLOR_TERMS = 6
HALO_CURVE = 64
HALO_PEER = 8
F32 = jnp.float32
BF16 = jnp.bfloat16
LANES = 128
FAR = 14
KB = 64


def up(n, m):
    return -(-n // m) * m


def halves(x):
    hi = x.astype(BF16)
    return hi, (x - hi.astype(F32)).astype(BF16)


def dot(a, b):
    return jnp.dot(a, b, preferred_element_type=F32)


class Dims:
    def __init__(self, basis, nvar, elements, fbasis, slots, subs):
        self.basis, self.nvar, self.elements, self.fbasis = basis, nvar, elements, fbasis
        self.slots, self.subs = slots, subs
        self.mp = up(fbasis, 8)
        self.fm = 4 * self.mp
        self.rows = nvar * self.mp
        self.width = nvar * elements
        self.cols4 = 4 * elements
        self.slot_cols = up(slots, LANES)
        self.half = up(-(-self.rows // 2), 8)
        self.rows_pad = up(self.rows, LANES)
        self.left_rows = self.fm + 3 * basis
        self.face_groups = [(r0, min(16, self.mp - r0)) for r0 in range(0, self.mp, 16)]
        self.chunks = []
        c0 = 0
        while c0 < self.width:
            cn = min(2 * elements, self.width - c0)
            self.chunks.append((c0, cn))
            c0 += cn

    def var(self, v):
        return slice(v * self.elements, (v + 1) * self.elements)


def fill_left(n, left, pad, project, mats):
    pad[...] = jnp.zeros_like(pad)
    for m in range(n.fbasis):
        for g in range(4):
            r = g * n.mp + m
            pad[r : r + 1, : n.basis] = project[m, g : g + 1, :]
    for d in range(3):
        r = n.fm + d * n.basis
        pad[r : r + n.basis, : n.basis] = mats[d]
    w = pad[...]
    hi = w.astype(BF16).astype(F32)
    lo = w - hi
    left[:, :LANES] = (hi + pltpu.roll(lo, KB, 1)).astype(BF16)
    left[:, LANES : LANES + KB] = hi[:, :KB].astype(BF16)


def put(n, right, r0, v, x):
    rows = x.shape[0]
    if rows % 16:
        x = jnp.concatenate([x, jnp.zeros((16 - rows % 16, x.shape[1]), F32)], axis=0)
        rows = x.shape[0]
    hi, lo = halves(x)
    c = n.var(v)
    right[r0 : r0 + rows, c] = hi
    right[KB + r0 : KB + r0 + rows, c] = hi
    right[2 * KB + r0 : 2 * KB + r0 + rows, c] = lo


def mix(n, load, terms, coef, outs=None):
    outs = range(n.nvar) if outs is None else outs
    acc = {}
    for v in range(n.nvar):
        for k in range(terms):
            t = load(v, k)
            for w in outs:
                p = t * coef(v, w, k)
                acc[w] = acc[w] + p if w in acc else p
    return acc


def spread_rows(n, spread, left, right, r, rows):
    for c0, cn in n.chunks:
        spread[r : r + rows, c0 : c0 + cn] = dot(left[r : r + rows, :], right[:, c0 : c0 + cn])


def block_of(n, c0, cn):
    return range(c0 // n.elements, (c0 + cn) // n.elements)


def star_mix(n, spread, star, outs):
    def load(v, d):
        r = n.fm + d * n.basis
        return spread[r : r + n.basis, n.var(v)]

    return mix(n, load, 3, lambda v, w, d: star[v, w, d : d + 1, :], outs)


def predict(n, left, right, spreads, star, sums, weights):
    def step(k, inv, two, now, later):
        inv = inv / (k + 1)
        two = two * 2.0
        scale = weights(inv, two)
        for c0, cn in n.chunks:
            for w, x in star_mix(n, now, star, block_of(n, c0, cn)).items():
                for field, s in zip(sums, scale):
                    field[:, n.var(w)] += s * x
                if later is not None:
                    put(n, right, 0, w, x)
            if later is not None:
                later[n.fm :, c0 : c0 + cn] = dot(left[n.fm :, :], right[:, c0 : c0 + cn])
        return inv, two

    def body(j, carry):
        k = (2 * j).astype(F32)
        carry = step(k + 1.0, *carry, spreads[0], spreads[1])
        return step(k + 2.0, *carry, spreads[1], spreads[0])

    spread_rows(n, spreads[0], left, right, n.fm, 3 * n.basis)
    steps = TAYLOR_TERMS - 1
    carry = lax.fori_loop(0, (steps - 1) // 2, body, (jnp.float32(1.0), jnp.float32(2.0)))
    step(float(steps), *carry, spreads[0], None)


def fill_right(n, right, field):
    for v in range(n.nvar):
        put(n, right, 0, v, field[:, n.var(v)])


def lane_pick(x, lanes):
    return jnp.take_along_axis(x, jnp.broadcast_to(lanes, x.shape), axis=1, mode="promise_in_bounds")


def face_pick(n, table, element, face):
    got = lane_pick(table[:, n.var(0)], element)
    for g in range(1, 4):
        got = jnp.where(face == g, lane_pick(table[:, n.var(g)], element), got)
    return got


def own_traces(n, table, index, face, f):
    idx = index[f : f + 1, :]
    return jnp.where(idx < n.elements, face_pick(n, table, idx & (n.elements - 1), face[f : f + 1, :]), 0.0)


def halo_slots(n, index, f):
    dom = lax.axis_index("dom")
    last = lax.axis_size("dom") - 1
    slot = index[f : f + 1, :] - n.elements
    slot = jnp.where(jnp.logical_and(slot < HALO_CURVE, dom == 0), -1, slot)
    high = jnp.logical_and(slot >= HALO_CURVE, slot < 2 * HALO_CURVE)
    return jnp.where(jnp.logical_and(high, dom == last), -1, slot)


def traces_and_sends(n, left, right, table, sends, turned, near, far, peers):
    for c0, cn in n.chunks:
        p = dot(left[: n.fm, :], right[:, c0 : c0 + cn])
        for v in range(c0 // n.elements, (c0 + cn) // n.elements):
            o = v * n.elements - c0
            for g in range(4):
                table[v * n.mp : (v + 1) * n.mp, n.var(g)] = p[g * n.mp : (g + 1) * n.mp, o : o + n.elements]
    chosen = [face_pick(n, table, sends[0:1, c : c + LANES], sends[1:2, c : c + LANES])
              for c in range(0, n.slot_cols, LANES)]
    curve = chosen[0]
    first, rest = curve[: n.half], curve[n.half :]
    short = n.half - rest.shape[0]
    if short:
        rest = jnp.concatenate([rest, jnp.zeros((short, LANES), F32)], axis=0)
    lane = lax.broadcasted_iota(jnp.int32, first.shape, 1)
    lower = jnp.where(lane < HALO_CURVE, first, pltpu.roll(rest, HALO_CURVE, 1))
    upper = jnp.where(lane < HALO_CURVE, pltpu.roll(first, HALO_CURVE, 1), rest)
    even = jnp.full(first.shape, lax.rem(lax.axis_index("dom"), 2), jnp.int32) == 0
    near[...] = jnp.where(even, upper, lower)
    far[...] = jnp.where(even, lower, upper)
    turned[...] = jnp.zeros_like(turned)
    wide = jnp.concatenate([jnp.concatenate(chosen[1:], axis=1), jnp.zeros((n.rows_pad - n.rows, n.slot_cols - LANES), F32)], axis=0)
    turned[...] = wide.T
    for k, ref in enumerate(peers):
        block = peer_block(n, k, False)
        ref[...] = turned[pl.ds(pl.multiple_of(block * HALO_PEER, HALO_PEER), HALO_PEER), :]


def first_kernel(n, *refs):
    brought = refs[:FAR]
    first, second, table, near, far = refs[FAR : FAR + 5]
    peers = refs[FAR + 5 : FAR + 5 + n.subs]
    left, sends = refs[FAR + 5 + n.subs : FAR + 7 + n.subs]
    kept = refs[FAR + 7 + n.subs : 2 * FAR + 5 + n.subs]
    right, spread, held, pad, turned, send_element, send_face, arrived = refs[2 * FAR + 5 + n.subs :]
    copies = [pltpu.make_async_copy(src, dst, arrived.at[i])
              for i, (src, dst) in enumerate(zip(brought, (send_element, send_face) + tuple(kept)))]
    for c in copies[2:6] + copies[:2]:
        c.start()
    project, stiffness, dof, star = kept[:4]
    for c in copies[2:4]:
        c.wait()
    fill_left(n, left, pad, project, [stiffness[d].T for d in range(3)])
    copies[4].wait()
    for v in range(n.nvar):
        x = dof[v]
        first[:, n.var(v)] = x
        second[:, n.var(v)] = x
    fill_right(n, right, first)
    for c in copies[:2]:
        c.wait()
    sends[...] = jnp.zeros_like(sends)
    sends[0:1, : n.slots] = send_element[...]
    sends[1:2, : n.slots] = send_face[...]
    copies[5].wait()
    for c in copies[6:]:
        c.start()
    predict(n, left, right, [spread, held], star, [first, second],
            lambda inv, two: [inv, (two - 1.0) * inv])
    fill_right(n, right, first)
    traces_and_sends(n, left, right, table, sends, turned, near, far, peers)
    for c in copies[6:]:
        c.wait()


def own_part(n, left, right, spread, star, flux_local, lift, solved, stacked, part):
    spread_rows(n, spread, left, right, 0, n.fm)
    for g in range(4):
        for r0, rn in n.face_groups:
            r = g * n.mp + r0

            def load(v, k, r=r, rn=rn):
                return spread[r : r + rn, n.var(v)]

            acc = mix(n, load, 1, lambda v, w, k, g=g: flux_local[v, w, g : g + 1, :])
            for w in range(n.nvar):
                solved[r : r + rn, n.var(w)] = acc[w]
    for w in range(n.nvar):
        hi, lo = halves(solved[:, n.var(w)])
        stacked[: n.fm, n.var(w)] = hi
        stacked[LANES : LANES + n.fm, n.var(w)] = lo
    stacked[n.fm : LANES, :] = jnp.zeros((LANES - n.fm, n.width), BF16)
    stacked[LANES + n.fm :, :] = jnp.zeros((LANES - n.fm, n.width), BF16)
    spread_rows(n, spread, left, right, n.fm, 3 * n.basis)
    for c0, cn in n.chunks:
        for w, x in star_mix(n, spread, star, block_of(n, c0, cn)).items():
            part[:, n.var(w)] = x
    for c0, cn in n.chunks:
        out = dot(lift[...], stacked[:, c0 : c0 + cn])
        part[:, c0 : c0 + cn] = part[:, c0 : c0 + cn] - (out[: n.basis] + out[n.basis :])


def lift_rows(n, out, tall, w):
    hi = w.astype(BF16).astype(F32)
    lo = w - hi
    span = w.shape[1]
    tall[: n.basis, :span] = hi
    tall[n.basis : 2 * n.basis, :span] = lo
    out[:, :span] = tall[: 2 * n.basis, :span].astype(BF16)
    tall[n.basis : 2 * n.basis, :span] = jnp.zeros_like(lo)
    out[:, span:] = tall[: 2 * n.basis, :span].astype(BF16)


def second_kernel(n, field, table, project, stiffness, star, face_lift, face_rotate, flux_local, index, face, orient,
                  part, found, left, lift, lift_turned, masks,
                  right, spread, pad, solved, stacked, wide, tall, square, mask_rows):
    fill_left(n, left, pad, project, [stiffness[d] for d in range(3)])
    fill_right(n, right, field)
    wide[...] = jnp.zeros_like(wide)
    square[...] = jnp.zeros_like(square)
    for m in range(n.fbasis):
        for g in range(4):
            r = g * n.mp + m
            square[r : r + 1, : n.basis] = face_lift[m, g : g + 1, :]
    base = square[...]
    lift_rows(n, lift, tall, base.T[: n.basis, :])
    for o in range(3):
        square[...] = jnp.zeros_like(square)
        square[: n.fbasis, : n.fbasis] = face_rotate[o]
        turn = square[...].T[: n.mp, :]
        turn = turn[:, : n.mp]
        for g in range(4):
            r = o * n.fm + g * n.mp
            wide[r : r + n.mp, :] = jnp.dot(turn, base[g * n.mp : (g + 1) * n.mp, :],
                                            precision=lax.Precision.HIGHEST, preferred_element_type=F32)
    blocks = wide.shape[0] // LANES
    turned = jnp.concatenate([wide[i * LANES : (i + 1) * LANES, :].T[: n.basis, :] for i in range(blocks)], axis=1)
    lift_rows(n, lift_turned, tall, turned)
    for f in range(4):
        for o in range(3):
            r = o * n.fm + f * n.mp
            mask_rows[r : r + n.mp, :] = jnp.broadcast_to(
                jnp.where(orient[f : f + 1, :] == o, 1.0, 0.0), (n.mp, n.elements))
    masks[...] = mask_rows[...].astype(BF16)
    own_part(n, left, right, spread, star, flux_local, lift, solved, stacked, part)
    for f in range(4):
        found[:, n.var(f)] = own_traces(n, table, index, face, f)


def neighbour_part(n, near, far, peers, found, index, flux_neighbour, masks,
                   traces, solved, stacked, turned):
    lane = lax.broadcasted_iota(jnp.int32, near.shape, 1)
    even = jnp.full(near.shape, lax.rem(lax.axis_index("dom"), 2), jnp.int32) == 0
    b = jnp.where(even, far[...], near[...])
    a = jnp.where(even, near[...], far[...])
    first = jnp.where(lane < HALO_CURVE, b, pltpu.roll(a, HALO_CURVE, 1))
    rest = jnp.where(lane < HALO_CURVE, pltpu.roll(b, HALO_CURVE, 1), a)
    curve = jnp.concatenate([first, rest], axis=0)[: n.rows]
    turned[...] = jnp.zeros_like(turned)
    for k, ref in enumerate(peers):
        block = peer_block(n, k, True)
        turned[pl.ds(pl.multiple_of(block * HALO_PEER, HALO_PEER), HALO_PEER), :] = ref[...]
    flat = turned[...].T[: n.rows, :]
    tiles = [curve] + [flat[:, c : c + LANES] for c in range(0, n.slot_cols - LANES, LANES)]
    for f in range(4):
        slot = halo_slots(n, index, f)
        got = 0.0
        for i, tile in enumerate(tiles):
            named = jnp.logical_and(slot >= i * LANES, slot < (i + 1) * LANES)
            got = jnp.where(named, lane_pick(tile, slot & (LANES - 1)), got)
        traces[:, n.var(f)] = found[:, n.var(f)] + got
        for r0, rn in n.face_groups:
            def load(v, k, f=f, r0=r0, rn=rn):
                return traces[v * n.mp + r0 : v * n.mp + r0 + rn, n.var(f)]

            acc = mix(n, load, 1, lambda v, w, k, f=f: flux_neighbour[v, w, f : f + 1, :])
            for w in range(n.nvar):
                solved[f * n.mp + r0 : f * n.mp + r0 + rn, n.var(w)] = acc[w]
    span = stacked.shape[0] // 2
    for w in range(n.nvar):
        hi, lo = halves(solved[:, n.var(w)])
        for o in range(3):
            m = masks[o * n.fm : (o + 1) * n.fm, :]
            stacked[o * n.fm : (o + 1) * n.fm, n.var(w)] = hi * m
            stacked[span + o * n.fm : span + (o + 1) * n.fm, n.var(w)] = lo * m
    gap = span - 3 * n.fm
    if gap:
        stacked[3 * n.fm : span, :] = jnp.zeros((gap, n.width), BF16)
        stacked[span + 3 * n.fm :, :] = jnp.zeros((gap, n.width), BF16)


def third_kernel(n, *refs):
    near, far = refs[:2]
    peers = refs[2 : 2 + n.subs]
    (found, index, flux_neighbour, masks, lift_turned, part, dof, labels, second, star, left, sends,
     later, middle, traces, table, near_out, far_out) = refs[2 + n.subs : 20 + n.subs]
    sent = refs[20 + n.subs : 20 + 2 * n.subs]
    right, spread, held, solved, stacked, turned = refs[20 + 2 * n.subs :]
    neighbour_part(n, near, far, peers, found, index, flux_neighbour, masks,
                   traces, solved, stacked, turned)
    fine = labels[...] == 0
    for c0, cn in n.chunks:
        out = dot(lift_turned[...], stacked[:, c0 : c0 + cn])
        nb = out[: n.basis] + out[n.basis :]
        for v in range(c0 // n.elements, (c0 + cn) // n.elements):
            c = n.var(v)
            o = v * n.elements - c0
            x = dof[v]
            mid = jnp.where(fine, x + (part[:, c] - nb[:, o : o + n.elements]), x)
            middle[:, c] = mid
            later[:, c] = mid
    fill_right(n, right, middle)
    predict(n, left, right, [spread, held], star, [later], lambda inv, two: [inv])
    for v in range(n.nvar):
        c = n.var(v)
        later[:, c] = jnp.where(fine, later[:, c], second[:, c])
    fill_right(n, right, later)
    traces_and_sends(n, left, right, table, sends, turned, near_out, far_out, sent)


def fourth_kernel(n, first, second, later, middle, labels, star, left, flux_local, lift, table, index, face, traces,
                  part, found, right, spread, solved, stacked):
    fine = labels[...] == 0
    for v in range(n.nvar):
        c = n.var(v)
        put(n, right, 0, v, jnp.where(fine, later[:, c], first[:, c] + second[:, c]))
    own_part(n, left, right, spread, star, flux_local, lift, solved, stacked, part)
    part[...] = middle[...] + part[...]
    for f in range(4):
        c = n.var(f)
        found[:, c] = own_traces(n, table, index, face, f) + jnp.where(fine, 0.0, traces[:, c])


def fifth_kernel(n, *refs):
    near, far = refs[:2]
    peers = refs[2 : 2 + n.subs]
    (found, index, flux_neighbour, masks, lift_turned, part, out,
     traces, solved, stacked, turned, result, left_for) = refs[2 + n.subs :]
    neighbour_part(n, near, far, peers, found, index, flux_neighbour, masks,
                   traces, solved, stacked, turned)
    copies = []
    for c0, cn in n.chunks:
        got = dot(lift_turned[...], stacked[:, c0 : c0 + cn])
        nb = got[: n.basis] + got[n.basis :]
        for v in range(c0 // n.elements, (c0 + cn) // n.elements):
            o = v * n.elements - c0
            result[v] = part[:, n.var(v)] - nb[:, o : o + n.elements]
            copies.append(pltpu.make_async_copy(result.at[v], out.at[v], left_for.at[v]))
            copies[-1].start()
    for c in copies:
        c.wait()


def call(kernel, n, operands, outs, scratch, far_in=False, far_out=False):
    near, far = pltpu.VMEM, pltpu.HBM
    place = far if far_in else near

    def body(*refs):
        kernel(n, *refs)

    return pl.pallas_call(
        body,
        out_shape=[(far if far_out else near)(s, t) for s, t in outs],
        in_specs=[pl.BlockSpec(memory_space=place)] * len(operands),
        out_specs=[pl.BlockSpec(memory_space=far if far_out else near)] * len(outs),
        scratch_shapes=scratch,
        compiler_params=pltpu.CompilerParams(vmem_limit_bytes=24 << 20),
    )(*[pltpu.with_memory_space_constraint(x, place) for x in operands])


def along(value, axis, partner):
    count = lax.axis_size(axis)
    pairs = [(i, partner(i)) for i in range(count)]
    return lax.ppermute(value, axis, [(i, j if 0 <= j < count else i) for i, j in pairs])


def exchange(near, far, peers):
    count = lax.axis_size("sub")
    swaps = count & (count - 1) == 0
    got = [peers[0]]
    far = along(far, "dom", lambda i: i + 1 if i % 2 else i - 1)
    for k, p in enumerate(peers):
        if k:
            got.append(along(p, "sub", lambda i, k=k: i ^ k if swaps else (i + k) % count))
    near = along(near, "dom", lambda i: i ^ 1)
    return [near, far] + got


def peer_block(n, k, back):
    here = lax.axis_index("sub")
    if n.subs & (n.subs - 1) == 0:
        return here ^ k
    return lax.rem(here + (n.subs - k if back else k), n.subs)


def per_device(dof_values, stiffness, face_project, face_lift, face_rotate, star_matrices, flux_local, flux_neighbour,
               cluster_labels, neighbour_index, neighbour_face, neighbour_orient, send_element, send_face):
    n = Dims(dof_values.shape[0], dof_values.shape[1], dof_values.shape[2], face_project.shape[1],
             send_element.shape[1], lax.axis_size("sub"))
    dof = jnp.transpose(dof_values, (1, 0, 2))
    star = jnp.transpose(star_matrices, (1, 2, 0, 3))
    local = jnp.transpose(flux_local, (1, 2, 0, 3))
    remote = jnp.transpose(flux_neighbour, (1, 2, 0, 3))
    project = jnp.transpose(face_project, (1, 0, 2))
    lift = jnp.transpose(face_lift, (2, 0, 1))
    labels = cluster_labels.reshape(1, n.elements)

    field = ((n.basis, n.width), F32)
    grid = ((n.rows, n.cols4), F32)
    pack = ((n.half, LANES), F32)
    peer = ((HALO_PEER, n.rows_pad), F32)
    left_t = ((n.left_rows, 3 * KB), BF16)
    rot_rows = up(3 * n.fm, LANES)
    right_t = pltpu.VMEM((3 * KB, n.width), BF16)
    spread_t = pltpu.VMEM((n.left_rows, n.width), F32)
    held_t = spread_t
    turned_t = pltpu.VMEM((n.slot_cols - LANES, n.rows_pad), F32)
    solved_t = pltpu.VMEM((n.fm, n.width), F32)
    own_stack = pltpu.VMEM((2 * LANES, n.width), BF16)
    rot_stack = pltpu.VMEM((2 * rot_rows, n.width), BF16)
    pad_t = pltpu.VMEM((n.left_rows, LANES), F32)

    slots = [send_element, send_face]
    kept = [project, stiffness, dof, star, lift, face_rotate, local, remote, labels,
            neighbour_index, neighbour_face, neighbour_orient]
    outs = call(
        first_kernel, n, slots + kept,
        [field, field, grid, pack, pack] + [peer] * n.subs + [left_t, ((8, n.slot_cols), jnp.int32)]
        + [(x.shape, x.dtype) for x in kept],
        [right_t, spread_t, held_t, pad_t, turned_t]
        + [pltpu.VMEM(x.shape, x.dtype) for x in slots] + [pltpu.SemaphoreType.DMA((FAR,))],
        far_in=True)
    first, second, table, near, far = outs[:5]
    peers = outs[5 : 5 + n.subs]
    left_one, sends = outs[5 + n.subs : 7 + n.subs]
    project, stiffness, dof, star, lift, face_rotate, local, remote, labels, index, face, orient = outs[7 + n.subs :]
    got = exchange(near, far, peers)
    part, found, left_two, lift_own, lift_rot, masks = call(
        second_kernel, n,
        [first, table, project, stiffness, star, lift, face_rotate, local, index, face, orient],
        [field, grid, left_t, ((2 * n.basis, 2 * LANES), BF16), ((2 * n.basis, 2 * rot_rows), BF16),
         ((3 * n.fm, n.elements), BF16)],
        [right_t, spread_t, pad_t, solved_t, own_stack]
        + [pltpu.VMEM(s, F32) for s in ((rot_rows, LANES), (2 * n.basis, rot_rows), (LANES, LANES), (3 * n.fm, n.elements))])
    outs = call(
        third_kernel, n,
        got + [found, index, remote, masks, lift_rot, part, dof, labels, second, star, left_one, sends],
        [field, field, grid, grid, pack, pack] + [peer] * n.subs,
        [right_t, spread_t, held_t, solved_t, rot_stack, turned_t])
    later, middle, traces, table, near, far = outs[:6]
    got = exchange(near, far, outs[6:])
    part, found = call(
        fourth_kernel, n,
        [first, second, later, middle, labels, star, left_two, local, lift_own, table, index, face, traces],
        [field, grid], [right_t, spread_t, solved_t, own_stack])
    (out,) = call(
        fifth_kernel, n, got + [found, index, remote, masks, lift_rot, part],
        [((n.nvar, n.basis, n.elements), F32)],
        [pltpu.VMEM(*grid), solved_t, rot_stack, turned_t, pltpu.VMEM((n.nvar, n.basis, n.elements), F32),
         pltpu.SemaphoreType.DMA((n.nvar,))], far_out=True)
    return jnp.transpose(out, (1, 0, 2))


def solution(mesh):
    cells = ("dom", "sub")
    in_specs = (
        P(None, None, cells),
        P(),
        P(),
        P(),
        P(),
        P(None, None, None, cells),
        P(None, None, None, cells),
        P(None, None, None, cells),
        P(cells),
        P(None, cells),
        P(None, cells),
        P(None, cells),
        P(cells, None),
        P(cells, None),
    )
    out_specs = P(None, None, cells)
    return jax.shard_map(per_device, mesh=mesh, in_specs=in_specs, out_specs=out_specs, check_vma=False)
```

```python
import jax
import jax.numpy as jnp
from jax import lax
from jax.experimental import pallas as pl
from jax.experimental.pallas import tpu as pltpu
from jax.sharding import PartitionSpec as P


TAYLOR_TERMS = 6
HALO_CURVE = 64
HALO_PEER = 8
F32 = jnp.float32
BF16 = jnp.bfloat16
LANES = 128
FAR = 14
KB = 64


def up(n, m):
    return -(-n // m) * m


def halves(x):
    hi = x.astype(BF16)
    return hi, (x - hi.astype(F32)).astype(BF16)


def dot(a, b):
    return jnp.dot(a, b, preferred_element_type=F32)


class Dims:
    def __init__(self, basis, nvar, elements, fbasis, slots, subs):
        self.basis, self.nvar, self.elements, self.fbasis = basis, nvar, elements, fbasis
        self.slots, self.subs = slots, subs
        self.mp = up(fbasis, 8)
        self.fm = 4 * self.mp
        self.rows = nvar * self.mp
        self.width = nvar * elements
        self.cols4 = 4 * elements
        self.slot_cols = up(slots, LANES)
        self.half = up(-(-self.rows // 2), 8)
        self.rows_pad = up(self.rows, LANES)
        self.left_rows = self.fm + 3 * basis
        self.face_groups = [(r0, min(16, self.mp - r0)) for r0 in range(0, self.mp, 16)]
        self.chunks = []
        c0 = 0
        while c0 < self.width:
            cn = min(2 * elements, self.width - c0)
            self.chunks.append((c0, cn))
            c0 += cn

    def var(self, v):
        return slice(v * self.elements, (v + 1) * self.elements)


def fill_left(n, left, pad, project, mats):
    pad[...] = jnp.zeros_like(pad)
    for m in range(n.fbasis):
        for g in range(4):
            r = g * n.mp + m
            pad[r : r + 1, : n.basis] = project[m, g : g + 1, :]
    for d in range(3):
        r = n.fm + d * n.basis
        pad[r : r + n.basis, : n.basis] = mats[d]
    w = pad[...]
    hi = w.astype(BF16).astype(F32)
    lo = w - hi
    left[:, :LANES] = (hi + pltpu.roll(lo, KB, 1)).astype(BF16)
    left[:, LANES : LANES + KB] = hi[:, :KB].astype(BF16)


def put(n, right, r0, v, x):
    rows = x.shape[0]
    if rows % 16:
        x = jnp.concatenate([x, jnp.zeros((16 - rows % 16, x.shape[1]), F32)], axis=0)
        rows = x.shape[0]
    hi, lo = halves(x)
    c = n.var(v)
    right[r0 : r0 + rows, c] = hi
    right[KB + r0 : KB + r0 + rows, c] = hi
    right[2 * KB + r0 : 2 * KB + r0 + rows, c] = lo


def mix(n, load, terms, coef, outs=None):
    outs = range(n.nvar) if outs is None else outs
    acc = {}
    for v in range(n.nvar):
        for k in range(terms):
            t = load(v, k)
            for w in outs:
                p = t * coef(v, w, k)
                acc[w] = acc[w] + p if w in acc else p
    return acc


def spread_rows(n, spread, left, right, r, rows):
    for c0, cn in n.chunks:
        spread[r : r + rows, c0 : c0 + cn] = dot(left[r : r + rows, :], right[:, c0 : c0 + cn])


def block_of(n, c0, cn):
    return range(c0 // n.elements, (c0 + cn) // n.elements)


def star_mix(n, spread, star, outs):
    def load(v, d):
        r = n.fm + d * n.basis
        return spread[r : r + n.basis, n.var(v)]

    return mix(n, load, 3, lambda v, w, d: star[v, w, d : d + 1, :], outs)


def predict(n, left, right, spreads, star, sums, weights):
    def step(k, inv, two, now, later):
        inv = inv / (k + 1)
        two = two * 2.0
        scale = weights(inv, two)
        for c0, cn in n.chunks:
            for w, x in star_mix(n, now, star, block_of(n, c0, cn)).items():
                for field, s in zip(sums, scale):
                    field[:, n.var(w)] += s * x
                if later is not None:
                    put(n, right, 0, w, x)
            if later is not None:
                later[n.fm :, c0 : c0 + cn] = dot(left[n.fm :, :], right[:, c0 : c0 + cn])
        return inv, two

    def body(j, carry):
        k = (2 * j).astype(F32)
        carry = step(k + 1.0, *carry, spreads[0], spreads[1])
        return step(k + 2.0, *carry, spreads[1], spreads[0])

    spread_rows(n, spreads[0], left, right, n.fm, 3 * n.basis)
    steps = TAYLOR_TERMS - 1
    carry = lax.fori_loop(0, (steps - 1) // 2, body, (jnp.float32(1.0), jnp.float32(2.0)))
    step(float(steps), *carry, spreads[0], None)


def fill_right(n, right, field):
    for v in range(n.nvar):
        put(n, right, 0, v, field[:, n.var(v)])


def lane_pick(x, lanes):
    return jnp.take_along_axis(x, jnp.broadcast_to(lanes, x.shape), axis=1, mode="promise_in_bounds")


def face_pick(n, table, element, face):
    got = lane_pick(table[:, n.var(0)], element)
    for g in range(1, 4):
        got = jnp.where(face == g, lane_pick(table[:, n.var(g)], element), got)
    return got


def own_traces(n, table, index, face, f):
    idx = index[f : f + 1, :]
    return jnp.where(idx < n.elements, face_pick(n, table, idx & (n.elements - 1), face[f : f + 1, :]), 0.0)


def halo_slots(n, index, f):
    dom = lax.axis_index("dom")
    last = lax.axis_size("dom") - 1
    slot = index[f : f + 1, :] - n.elements
    slot = jnp.where(jnp.logical_and(slot < HALO_CURVE, dom == 0), -1, slot)
    high = jnp.logical_and(slot >= HALO_CURVE, slot < 2 * HALO_CURVE)
    return jnp.where(jnp.logical_and(high, dom == last), -1, slot)


def traces_and_sends(n, left, right, table, sends, turned, near, far, peers):
    for c0, cn in n.chunks:
        p = dot(left[: n.fm, :], right[:, c0 : c0 + cn])
        for v in range(c0 // n.elements, (c0 + cn) // n.elements):
            o = v * n.elements - c0
            for g in range(4):
                table[v * n.mp : (v + 1) * n.mp, n.var(g)] = p[g * n.mp : (g + 1) * n.mp, o : o + n.elements]
    chosen = [face_pick(n, table, sends[0:1, c : c + LANES], sends[1:2, c : c + LANES])
              for c in range(0, n.slot_cols, LANES)]
    curve = chosen[0]
    first, rest = curve[: n.half], curve[n.half :]
    short = n.half - rest.shape[0]
    if short:
        rest = jnp.concatenate([rest, jnp.zeros((short, LANES), F32)], axis=0)
    lane = lax.broadcasted_iota(jnp.int32, first.shape, 1)
    lower = jnp.where(lane < HALO_CURVE, first, pltpu.roll(rest, HALO_CURVE, 1))
    upper = jnp.where(lane < HALO_CURVE, pltpu.roll(first, HALO_CURVE, 1), rest)
    even = jnp.full(first.shape, lax.rem(lax.axis_index("dom"), 2), jnp.int32) == 0
    near[...] = jnp.where(even, upper, lower)
    far[...] = jnp.where(even, lower, upper)
    turned[...] = jnp.zeros_like(turned)
    wide = jnp.concatenate([jnp.concatenate(chosen[1:], axis=1), jnp.zeros((n.rows_pad - n.rows, n.slot_cols - LANES), F32)], axis=0)
    turned[...] = wide.T
    for k, ref in enumerate(peers):
        block = peer_block(n, k, False)
        ref[...] = turned[pl.ds(pl.multiple_of(block * HALO_PEER, HALO_PEER), HALO_PEER), :]


def first_kernel(n, *refs):
    brought = refs[:FAR]
    first, second, table, near, far = refs[FAR : FAR + 5]
    peers = refs[FAR + 5 : FAR + 5 + n.subs]
    left, sends = refs[FAR + 5 + n.subs : FAR + 7 + n.subs]
    kept = refs[FAR + 7 + n.subs : 2 * FAR + 5 + n.subs]
    right, spread, held, pad, turned, send_element, send_face, arrived = refs[2 * FAR + 5 + n.subs :]
    copies = [pltpu.make_async_copy(src, dst, arrived.at[i])
              for i, (src, dst) in enumerate(zip(brought, (send_element, send_face) + tuple(kept)))]
    for c in copies[2:6] + copies[:2]:
        c.start()
    project, stiffness, dof, star = kept[:4]
    for c in copies[2:4]:
        c.wait()
    fill_left(n, left, pad, project, [stiffness[d].T for d in range(3)])
    copies[4].wait()
    for v in range(n.nvar):
        x = dof[v]
        first[:, n.var(v)] = x
        second[:, n.var(v)] = x
    fill_right(n, right, first)
    for c in copies[:2]:
        c.wait()
    sends[...] = jnp.zeros_like(sends)
    sends[0:1, : n.slots] = send_element[...]
    sends[1:2, : n.slots] = send_face[...]
    copies[5].wait()
    for c in copies[6:]:
        c.start()
    predict(n, left, right, [spread, held], star, [first, second],
            lambda inv, two: [inv, (two - 1.0) * inv])
    fill_right(n, right, first)
    traces_and_sends(n, left, right, table, sends, turned, near, far, peers)
    for c in copies[6:]:
        c.wait()


def own_part(n, left, right, spread, star, flux_local, lift, solved, stacked, part):
    spread_rows(n, spread, left, right, 0, n.fm)
    for g in range(4):
        for r0, rn in n.face_groups:
            r = g * n.mp + r0

            def load(v, k, r=r, rn=rn):
                return spread[r : r + rn, n.var(v)]

            acc = mix(n, load, 1, lambda v, w, k, g=g: flux_local[v, w, g : g + 1, :])
            for w in range(n.nvar):
                solved[r : r + rn, n.var(w)] = acc[w]
    for w in range(n.nvar):
        hi, lo = halves(solved[:, n.var(w)])
        stacked[: n.fm, n.var(w)] = hi
        stacked[LANES : LANES + n.fm, n.var(w)] = lo
    stacked[n.fm : LANES, :] = jnp.zeros((LANES - n.fm, n.width), BF16)
    stacked[LANES + n.fm :, :] = jnp.zeros((LANES - n.fm, n.width), BF16)
    spread_rows(n, spread, left, right, n.fm, 3 * n.basis)
    for c0, cn in n.chunks:
        for w, x in star_mix(n, spread, star, block_of(n, c0, cn)).items():
            part[:, n.var(w)] = x
    for c0, cn in n.chunks:
        out = dot(lift[...], stacked[:, c0 : c0 + cn])
        part[:, c0 : c0 + cn] = part[:, c0 : c0 + cn] - (out[: n.basis] + out[n.basis :])


def lift_rows(n, out, tall, w):
    hi = w.astype(BF16).astype(F32)
    lo = w - hi
    span = w.shape[1]
    tall[: n.basis, :span] = hi
    tall[n.basis : 2 * n.basis, :span] = lo
    out[:, :span] = tall[: 2 * n.basis, :span].astype(BF16)
    tall[n.basis : 2 * n.basis, :span] = jnp.zeros_like(lo)
    out[:, span:] = tall[: 2 * n.basis, :span].astype(BF16)


def second_kernel(n, field, table, project, stiffness, star, face_lift, face_rotate, flux_local, index, face, orient,
                  part, found, left, lift, lift_turned, masks,
                  right, spread, pad, solved, stacked, wide, tall, square, mask_rows):
    fill_left(n, left, pad, project, [stiffness[d] for d in range(3)])
    fill_right(n, right, field)
    wide[...] = jnp.zeros_like(wide)
    square[...] = jnp.zeros_like(square)
    for m in range(n.fbasis):
        for g in range(4):
            r = g * n.mp + m
            square[r : r + 1, : n.basis] = face_lift[m, g : g + 1, :]
    base = square[...]
    lift_rows(n, lift, tall, base.T[: n.basis, :])
    for o in range(3):
        square[...] = jnp.zeros_like(square)
        square[: n.fbasis, : n.fbasis] = face_rotate[o]
        tall[o * n.mp : (o + 1) * n.mp, :LANES] = square[...].T[: n.mp, :]
    turn_hi, turn_lo = halves(tall[: 3 * n.mp, : n.mp])
    side = jnp.concatenate([base[g * n.mp : (g + 1) * n.mp, :] for g in range(4)], axis=1)
    side_hi, side_lo = halves(side)
    both = dot(turn_hi, side_hi) + (dot(turn_lo, side_hi) + dot(turn_hi, side_lo))
    for o in range(3):
        for g in range(4):
            r = o * n.fm + g * n.mp
            wide[r : r + n.mp, :] = both[o * n.mp : (o + 1) * n.mp, g * LANES : (g + 1) * LANES]
    blocks = wide.shape[0] // LANES
    turned = jnp.concatenate([wide[i * LANES : (i + 1) * LANES, :].T[: n.basis, :] for i in range(blocks)], axis=1)
    lift_rows(n, lift_turned, tall, turned)
    for f in range(4):
        for o in range(3):
            r = o * n.fm + f * n.mp
            mask_rows[r : r + n.mp, :] = jnp.broadcast_to(
                jnp.where(orient[f : f + 1, :] == o, 1.0, 0.0), (n.mp, n.elements))
    masks[...] = mask_rows[...].astype(BF16)
    own_part(n, left, right, spread, star, flux_local, lift, solved, stacked, part)
    for f in range(4):
        found[:, n.var(f)] = own_traces(n, table, index, face, f)


def neighbour_part(n, near, far, peers, found, index, flux_neighbour, masks,
                   traces, solved, stacked, turned):
    lane = lax.broadcasted_iota(jnp.int32, near.shape, 1)
    even = jnp.full(near.shape, lax.rem(lax.axis_index("dom"), 2), jnp.int32) == 0
    b = jnp.where(even, far[...], near[...])
    a = jnp.where(even, near[...], far[...])
    first = jnp.where(lane < HALO_CURVE, b, pltpu.roll(a, HALO_CURVE, 1))
    rest = jnp.where(lane < HALO_CURVE, pltpu.roll(b, HALO_CURVE, 1), a)
    curve = jnp.concatenate([first, rest], axis=0)[: n.rows]
    turned[...] = jnp.zeros_like(turned)
    for k, ref in enumerate(peers):
        block = peer_block(n, k, True)
        turned[pl.ds(pl.multiple_of(block * HALO_PEER, HALO_PEER), HALO_PEER), :] = ref[...]
    flat = turned[...].T[: n.rows, :]
    tiles = [curve] + [flat[:, c : c + LANES] for c in range(0, n.slot_cols - LANES, LANES)]
    for f in range(4):
        slot = halo_slots(n, index, f)
        got = 0.0
        for i, tile in enumerate(tiles):
            named = jnp.logical_and(slot >= i * LANES, slot < (i + 1) * LANES)
            got = jnp.where(named, lane_pick(tile, slot & (LANES - 1)), got)
        traces[:, n.var(f)] = found[:, n.var(f)] + got
        for r0, rn in n.face_groups:
            def load(v, k, f=f, r0=r0, rn=rn):
                return traces[v * n.mp + r0 : v * n.mp + r0 + rn, n.var(f)]

            acc = mix(n, load, 1, lambda v, w, k, f=f: flux_neighbour[v, w, f : f + 1, :])
            for w in range(n.nvar):
                solved[f * n.mp + r0 : f * n.mp + r0 + rn, n.var(w)] = acc[w]
    span = stacked.shape[0] // 2
    for w in range(n.nvar):
        hi, lo = halves(solved[:, n.var(w)])
        for o in range(3):
            m = masks[o * n.fm : (o + 1) * n.fm, :]
            stacked[o * n.fm : (o + 1) * n.fm, n.var(w)] = hi * m
            stacked[span + o * n.fm : span + (o + 1) * n.fm, n.var(w)] = lo * m
    gap = span - 3 * n.fm
    if gap:
        stacked[3 * n.fm : span, :] = jnp.zeros((gap, n.width), BF16)
        stacked[span + 3 * n.fm :, :] = jnp.zeros((gap, n.width), BF16)


def third_kernel(n, *refs):
    near, far = refs[:2]
    peers = refs[2 : 2 + n.subs]
    (found, index, flux_neighbour, masks, lift_turned, part, dof, labels, second, star, left, sends,
     later, middle, traces, table, near_out, far_out) = refs[2 + n.subs : 20 + n.subs]
    sent = refs[20 + n.subs : 20 + 2 * n.subs]
    right, spread, held, solved, stacked, turned = refs[20 + 2 * n.subs :]
    neighbour_part(n, near, far, peers, found, index, flux_neighbour, masks,
                   traces, solved, stacked, turned)
    fine = labels[...] == 0
    for c0, cn in n.chunks:
        out = dot(lift_turned[...], stacked[:, c0 : c0 + cn])
        nb = out[: n.basis] + out[n.basis :]
        for v in range(c0 // n.elements, (c0 + cn) // n.elements):
            c = n.var(v)
            o = v * n.elements - c0
            x = dof[v]
            mid = jnp.where(fine, x + (part[:, c] - nb[:, o : o + n.elements]), x)
            middle[:, c] = mid
            later[:, c] = mid
    fill_right(n, right, middle)
    predict(n, left, right, [spread, held], star, [later], lambda inv, two: [inv])
    for v in range(n.nvar):
        c = n.var(v)
        later[:, c] = jnp.where(fine, later[:, c], second[:, c])
    fill_right(n, right, later)
    traces_and_sends(n, left, right, table, sends, turned, near_out, far_out, sent)


def fourth_kernel(n, first, second, later, middle, labels, star, left, flux_local, lift, table, index, face, traces,
                  part, found, right, spread, solved, stacked):
    fine = labels[...] == 0
    for v in range(n.nvar):
        c = n.var(v)
        put(n, right, 0, v, jnp.where(fine, later[:, c], first[:, c] + second[:, c]))
    own_part(n, left, right, spread, star, flux_local, lift, solved, stacked, part)
    part[...] = middle[...] + part[...]
    for f in range(4):
        c = n.var(f)
        found[:, c] = own_traces(n, table, index, face, f) + jnp.where(fine, 0.0, traces[:, c])


def fifth_kernel(n, *refs):
    near, far = refs[:2]
    peers = refs[2 : 2 + n.subs]
    (found, index, flux_neighbour, masks, lift_turned, part, out,
     traces, solved, stacked, turned, result, left_for) = refs[2 + n.subs :]
    neighbour_part(n, near, far, peers, found, index, flux_neighbour, masks,
                   traces, solved, stacked, turned)
    copies = []
    for c0, cn in n.chunks:
        got = dot(lift_turned[...], stacked[:, c0 : c0 + cn])
        nb = got[: n.basis] + got[n.basis :]
        for v in range(c0 // n.elements, (c0 + cn) // n.elements):
            o = v * n.elements - c0
            result[v] = part[:, n.var(v)] - nb[:, o : o + n.elements]
            copies.append(pltpu.make_async_copy(result.at[v], out.at[v], left_for.at[v]))
            copies[-1].start()
    for c in copies:
        c.wait()


def call(kernel, n, operands, outs, scratch, far_in=False, far_out=False):
    near, far = pltpu.VMEM, pltpu.HBM
    place = far if far_in else near

    def body(*refs):
        kernel(n, *refs)

    return pl.pallas_call(
        body,
        out_shape=[(far if far_out else near)(s, t) for s, t in outs],
        in_specs=[pl.BlockSpec(memory_space=place)] * len(operands),
        out_specs=[pl.BlockSpec(memory_space=far if far_out else near)] * len(outs),
        scratch_shapes=scratch,
        compiler_params=pltpu.CompilerParams(vmem_limit_bytes=24 << 20),
    )(*[pltpu.with_memory_space_constraint(x, place) for x in operands])


def along(value, axis, partner):
    count = lax.axis_size(axis)
    pairs = [(i, partner(i)) for i in range(count)]
    return lax.ppermute(value, axis, [(i, j if 0 <= j < count else i) for i, j in pairs])


def exchange(near, far, peers):
    count = lax.axis_size("sub")
    swaps = count & (count - 1) == 0
    got = [peers[0]]
    far = along(far, "dom", lambda i: i + 1 if i % 2 else i - 1)
    for k, p in enumerate(peers):
        if k:
            got.append(along(p, "sub", lambda i, k=k: i ^ k if swaps else (i + k) % count))
    near = along(near, "dom", lambda i: i ^ 1)
    return [near, far] + got


def peer_block(n, k, back):
    here = lax.axis_index("sub")
    if n.subs & (n.subs - 1) == 0:
        return here ^ k
    return lax.rem(here + (n.subs - k if back else k), n.subs)


def per_device(dof_values, stiffness, face_project, face_lift, face_rotate, star_matrices, flux_local, flux_neighbour,
               cluster_labels, neighbour_index, neighbour_face, neighbour_orient, send_element, send_face):
    n = Dims(dof_values.shape[0], dof_values.shape[1], dof_values.shape[2], face_project.shape[1],
             send_element.shape[1], lax.axis_size("sub"))
    dof = jnp.transpose(dof_values, (1, 0, 2))
    star = jnp.transpose(star_matrices, (1, 2, 0, 3))
    local = jnp.transpose(flux_local, (1, 2, 0, 3))
    remote = jnp.transpose(flux_neighbour, (1, 2, 0, 3))
    project = jnp.transpose(face_project, (1, 0, 2))
    lift = jnp.transpose(face_lift, (2, 0, 1))
    labels = cluster_labels.reshape(1, n.elements)

    field = ((n.basis, n.width), F32)
    grid = ((n.rows, n.cols4), F32)
    pack = ((n.half, LANES), F32)
    peer = ((HALO_PEER, n.rows_pad), F32)
    left_t = ((n.left_rows, 3 * KB), BF16)
    rot_rows = up(3 * n.fm, LANES)
    right_t = pltpu.VMEM((3 * KB, n.width), BF16)
    spread_t = pltpu.VMEM((n.left_rows, n.width), F32)
    held_t = spread_t
    turned_t = pltpu.VMEM((n.slot_cols - LANES, n.rows_pad), F32)
    solved_t = pltpu.VMEM((n.fm, n.width), F32)
    own_stack = pltpu.VMEM((2 * LANES, n.width), BF16)
    rot_stack = pltpu.VMEM((2 * rot_rows, n.width), BF16)
    pad_t = pltpu.VMEM((n.left_rows, LANES), F32)

    slots = [send_element, send_face]
    kept = [project, stiffness, dof, star, lift, face_rotate, local, remote, labels,
            neighbour_index, neighbour_face, neighbour_orient]
    outs = call(
        first_kernel, n, slots + kept,
        [field, field, grid, pack, pack] + [peer] * n.subs + [left_t, ((8, n.slot_cols), jnp.int32)]
        + [(x.shape, x.dtype) for x in kept],
        [right_t, spread_t, held_t, pad_t, turned_t]
        + [pltpu.VMEM(x.shape, x.dtype) for x in slots] + [pltpu.SemaphoreType.DMA((FAR,))],
        far_in=True)
    first, second, table, near, far = outs[:5]
    peers = outs[5 : 5 + n.subs]
    left_one, sends = outs[5 + n.subs : 7 + n.subs]
    project, stiffness, dof, star, lift, face_rotate, local, remote, labels, index, face, orient = outs[7 + n.subs :]
    got = exchange(near, far, peers)
    part, found, left_two, lift_own, lift_rot, masks = call(
        second_kernel, n,
        [first, table, project, stiffness, star, lift, face_rotate, local, index, face, orient],
        [field, grid, left_t, ((2 * n.basis, 2 * LANES), BF16), ((2 * n.basis, 2 * rot_rows), BF16),
         ((3 * n.fm, n.elements), BF16)],
        [right_t, spread_t, pad_t, solved_t, own_stack]
        + [pltpu.VMEM(s, F32) for s in ((rot_rows, LANES), (2 * n.basis, rot_rows), (LANES, LANES), (3 * n.fm, n.elements))])
    outs = call(
        third_kernel, n,
        got + [found, index, remote, masks, lift_rot, part, dof, labels, second, star, left_one, sends],
        [field, field, grid, grid, pack, pack] + [peer] * n.subs,
        [right_t, spread_t, held_t, solved_t, rot_stack, turned_t])
    later, middle, traces, table, near, far = outs[:6]
    got = exchange(near, far, outs[6:])
    part, found = call(
        fourth_kernel, n,
        [first, second, later, middle, labels, star, left_two, local, lift_own, table, index, face, traces],
        [field, grid], [right_t, spread_t, solved_t, own_stack])
    (out,) = call(
        fifth_kernel, n, got + [found, index, remote, masks, lift_rot, part],
        [((n.nvar, n.basis, n.elements), F32)],
        [pltpu.VMEM(*grid), solved_t, rot_stack, turned_t, pltpu.VMEM((n.nvar, n.basis, n.elements), F32),
         pltpu.SemaphoreType.DMA((n.nvar,))], far_out=True)
    return jnp.transpose(out, (1, 0, 2))


def solution(mesh):
    cells = ("dom", "sub")
    in_specs = (
        P(None, None, cells),
        P(),
        P(),
        P(),
        P(),
        P(None, None, None, cells),
        P(None, None, None, cells),
        P(None, None, None, cells),
        P(cells),
        P(None, cells),
        P(None, cells),
        P(None, cells),
        P(cells, None),
        P(cells, None),
    )
    out_specs = P(None, None, cells)
    return jax.shard_map(per_device, mesh=mesh, in_specs=in_specs, out_specs=out_specs, check_vma=False)
```
